128 devices in a mesh: seq: 16 (over x, z), head: 8 (over y, core).
Axes of the slice: x: 4, y: 4, z: 4, core: 2. Of those that a mesh axis runs over, the one named last changes fastest.
Arguments:
- hidden: bfloat16 [16, 1536, 2560], P('seq', 'head'), may hold values from -6 to 6
- norm_gain: float32 [2560], replicated, may hold values from 0.1 to 1.9
- w_qkv: bfloat16 [2560, 3840], P('seq'), may hold values from -0.15625 to 0.15625
- w_out: bfloat16 [2560, 2560], P(None, 'seq'), may hold values from -0.625 to 0.625
- kv_cache: bfloat16 [16, 4096, 1280], P('seq', None, 'head'), as said below
- new_len: int32 [16], replicated, may hold values from 1 to 1536, 12288 in all
- prefix_len: int32 [16], replicated, may hold values from 0 to 12287
Outputs:
- attn_out: bfloat16 [16, 1536, 2560], P('seq', 'head')
- kv_written: bfloat16 [16, 1536, 1280], P('seq', None, 'head')
The draws below stay inside these ranges and needn't reach their ends.
Inputs may be any that keep to these rules, and one draw needn't show every extreme that they name: `new_len`: the lengths sum to 12288 and the largest is 1536. `kv_cache`: keys are stored already rotated to their positions.
All inputs are finite; a program needn't handle non-finite values.
Results may differ from the reference program's by a relative error of at most 0.008.
The reference program's roundings to bfloat16 on the way (of `normed`, `probabilities` and `attended`) count: a program that leaves them out, or rounds other values in their place, can miss the bound.
Values may be sent and summed in bfloat16 or wider, within the bound.
A program may use at most 128 MiB of HBM per device.

```python
import math
import jax
import jax.numpy as jnp
import numpy as np
from jax import lax

D = 2560
Q_HEADS = 32
KV_HEADS = 8
HEAD_DIM = 80
WINDOW = 4096
GROUP = 4
REQS = 16
NEW_REQ = 1536


def draw_kv_cache(key, part):
    columns = 2 * KV_HEADS * HEAD_DIM
    drawn = 1.4 * jnp.clip(jax.random.normal(key, (REQS, WINDOW, columns), jnp.float32), -6.0, 6.0)
    return drawn.astype(jnp.bfloat16)


def with_ends(values, stream_key, least, largest):
    shape = values.shape
    place = [jax.random.randint(jax.random.fold_in(stream_key, axis), (), 0, shape[axis]) for axis in range(len(shape))]
    values = values.at[tuple(place)].set(least)
    longest = shape.index(max(shape))
    place[longest] = (place[longest] + 1) % shape[longest]
    return values.at[tuple(place)].set(largest)


def shard_levels(stream_key, extent, pieces, smallest, largest):
    level, own = 1.0, jax.random.fold_in(stream_key, 6)
    for dim, shards_of in pieces:
        heights = jnp.exp(jax.random.uniform(jax.random.fold_in(own, dim), (shards_of,), jnp.float32, smallest / len(pieces), largest / len(pieces)))
        level = level * jnp.repeat(heights, extent[dim] // shards_of).reshape([-1 if axis == dim else 1 for axis in range(len(extent))])
    return level


def profile(count, total, reach, skew):
    weights = [(1 << 20) // math.isqrt(grade ** skew) + 1 for grade in range(2, count + 1)]
    spare, given = total - reach - (count - 1), [1] * (count - 1)
    while spare > 0:
        candidates = [i for i in range(count - 1) if given[i] < reach]
        whole, budget = sum([weights[i] for i in candidates]), spare
        for i in candidates:
            addition = min(reach - given[i], max(1, budget * weights[i] // whole), spare)
            given[i] = given[i] + addition
            spare = spare - addition
    return np.array([reach] + given)


def ragged(stream_key, number_of, total, reach, slope):
    if number_of == 2:
        one = jax.random.randint(stream_key, (), max(1, total - reach), min(reach, total - 1) + 1)
        return jnp.stack([one, total - one])
    sizes = jnp.asarray(profile(number_of, total, reach, slope), jnp.int32)
    pairs = (number_of - 1) // 2
    giver, sink = sizes[1:1 + 2 * pairs:2], sizes[2:2 + 2 * pairs:2]
    margin = jnp.minimum(giver - 1, reach - sink)
    shifted = jax.random.randint(jax.random.fold_in(stream_key, 1), (pairs,), 0, 1 << 20) % (margin + 1)
    sizes = sizes.at[1:1 + 2 * pairs:2].set(giver - shifted).at[2:2 + 2 * pairs:2].set(sink + shifted)
    return sizes[jax.random.permutation(jax.random.fold_in(stream_key, 2), number_of)]


def normal_values(own_key, dims, deviation, limit, shards=(), kind=jnp.bfloat16):
    array = jax.random.normal(own_key, dims, jnp.float32) * deviation
    if len(shards) > 0:
        array = shard_levels(own_key, dims, shards, -0.22, 0.18) * array
    return jnp.clip(array, min=-limit, max=limit).astype(kind)


def setup_inputs(seed: int = 0) -> dict:
    arg_keys = jax.random.split(jax.random.key(seed), 8)
    hidden = normal_values(arg_keys[0], (REQS, NEW_REQ, D), 1.0, 6.0, ((0, 16), (1, 8)))
    norm_gain = jnp.clip(1.0 + 0.18 * jax.random.normal(arg_keys[1], (D,), jnp.float32), 0.1, 1.9)
    w_qkv = normal_values(arg_keys[2], (D, KV_HEADS * (GROUP + 2) * HEAD_DIM), (D // 2) ** -0.5, 0.15625, ((0, 16),))
    w_out = normal_values(arg_keys[3], (Q_HEADS * HEAD_DIM, D), (Q_HEADS * HEAD_DIM // 32) ** -0.5, 0.625, ((1, 16),))
    kv_cache = draw_kv_cache(jax.random.fold_in(arg_keys[7], 71), 0)
    new_len = ragged(arg_keys[5], REQS, REQS * NEW_REQ // 2, NEW_REQ, 2).astype(jnp.int32)
    prefix_len = with_ends(jax.random.randint(arg_keys[6], (REQS,), 0, 3 * WINDOW), jax.random.fold_in(arg_keys[6], 1), 0, (3 * WINDOW) - 1).astype(jnp.int32)
    return dict(hidden=hidden, norm_gain=norm_gain, w_qkv=w_qkv, w_out=w_out, kv_cache=kv_cache, new_len=new_len, prefix_len=prefix_len)


def normalize(hidden, norm_gain):
    values = hidden.astype(jnp.float32)
    meansq = lax.optimization_barrier(jnp.mean(values * values, axis=-1, keepdims=True))
    return (values * lax.rsqrt(meansq + 1e-05) * norm_gain).astype(jnp.bfloat16)

def rotate(values, position):
    halfway = values.shape[-1] // 2
    frequency = jnp.exp(jnp.arange(halfway, dtype=jnp.float32) * (-2.0 * math.log(10000.0) / values.shape[-1]))
    angles = position.astype(jnp.float32)[..., None] * frequency
    cosine = jnp.cos(angles)
    sine_part = jnp.sin(angles)
    leading = values[..., :halfway]
    trailing = values[..., halfway:]
    return jnp.concatenate([leading * cosine - trailing * sine_part, trailing * cosine + leading * sine_part], axis=-1)

def reference(hidden, norm_gain, w_qkv, w_out, kv_cache, new_len, prefix_len):
    score_scale = 1.0 / math.sqrt(HEAD_DIM)

    def one_request(request_items):
        tokens, length, prefix, cache_rows = request_items
        normed = normalize(tokens, norm_gain)
        projected = jnp.dot(normed, w_qkv, preferred_element_type=jnp.float32)
        projected = projected.reshape(NEW_REQ, KV_HEADS, GROUP + 2, HEAD_DIM)
        new_index = jnp.arange(NEW_REQ, dtype=jnp.int32)
        position = prefix + new_index
        queries = rotate(projected[:, :, :GROUP], position[:, None, None]).astype(jnp.bfloat16)
        keys_new = rotate(projected[:, :, GROUP], position[:, None]).astype(jnp.bfloat16)
        values_new = projected[:, :, GROUP + 1].astype(jnp.bfloat16)
        live_rows = new_index < length
        written = jnp.stack([keys_new, values_new], axis=2)
        written = jnp.where(live_rows[:, None, None, None], written, jnp.zeros_like(written))
        written = written.reshape(NEW_REQ, KV_HEADS * 2 * HEAD_DIM)
        cached = cache_rows.reshape(WINDOW, KV_HEADS, 2, HEAD_DIM)
        keys_all = jnp.concatenate([cached[:, :, 0], keys_new], axis=0)
        values_all = jnp.concatenate([cached[:, :, 1], values_new], axis=0)
        key_slot = jnp.arange(WINDOW + NEW_REQ, dtype=jnp.int32)
        allowed = (key_slot[None, :] > new_index[:, None]) & (key_slot[None, :] <= new_index[:, None] + WINDOW) & (key_slot[None, :] >= WINDOW - prefix)

        def one_head(head_items):
            head_queries, head_keys, head_values = head_items
            scores = jnp.einsum('qgd,kd->gqk', head_queries.astype(jnp.float32), head_keys.astype(jnp.float32)) * score_scale
            scores = jnp.where(allowed[None], scores, -jnp.inf)
            row_max = lax.optimization_barrier(jnp.max(scores, axis=-1, keepdims=True))
            weights = jnp.exp(scores - row_max)
            probabilities = (weights / lax.optimization_barrier(jnp.sum(weights, axis=-1, keepdims=True))).astype(jnp.bfloat16)
            return jnp.einsum('gqk,kd->qgd', probabilities.astype(jnp.float32), head_values.astype(jnp.float32))
        attended = lax.map(one_head, (jnp.transpose(queries, (1, 0, 2, 3)), jnp.transpose(keys_all, (1, 0, 2)), jnp.transpose(values_all, (1, 0, 2))))
        attended = jnp.transpose(attended, (1, 0, 2, 3))
        attended = jnp.where(live_rows[:, None, None, None], attended, 0.0).astype(jnp.bfloat16)
        attended = attended.reshape(NEW_REQ, Q_HEADS * HEAD_DIM)
        output = jnp.dot(attended, w_out, preferred_element_type=jnp.float32).astype(jnp.bfloat16)
        return (output, written)
    attn_out, kv_written = lax.map(one_request, (hidden, new_len, prefix_len, kv_cache))
    return (attn_out, kv_written)
```

```python
import math

import jax
import jax.numpy as jnp
import numpy as np
from jax import lax
from jax.experimental import pallas as pl
from jax.experimental.pallas import tpu as pltpu
from jax.sharding import PartitionSpec as P

HEAD_DIM = 80
HALF = HEAD_DIM // 2
GROUP = 4
WINDOW = 4096
QBLOCK = 128
HIDE = -(2.0**127)
F32 = jnp.float32
BF16 = jnp.bfloat16
MESH = pl.DeviceIdType.MESH


def matmul(a, b):
    return lax.dot_general(a, b, (((1,), (0,)), ((), ())), preferred_element_type=F32)


def kernel(
    hidden, gain, w_mine, wo_mine, kv, cos_slot, sin_slot, cos_pre, sin_pre, new_len, prefix_len,
    out, written,
    rows, wq, wo, keys, vals, queries, state, maxes, ready, landed, finished,
    w_send, w_recv, o_send, o_recv, p_send, p_recv, y_send, y_recv, a_send, a_recv,
):
    s = lax.axis_index("seq")
    h = lax.axis_index("head")
    y, c = h // 2, h % 2
    own = hidden.shape[0]
    chip = 2 * own
    width = hidden.shape[1]
    piece = w_mine.shape[0]
    half_o = piece // 2
    length, prefix = new_len[s], prefix_len[s]
    x, z = s // 4, s % 4
    a, b = x + c * (z - x), z + c * (x - z)
    step_a, step_b = 4 - 3 * c, 1 + 3 * c

    def slot(da, db):
        return lax.rem(a + da + 4, 4) * step_a + lax.rem(b + db + 4, 4) * step_b

    def head_of(dy, core):
        return lax.rem(y + dy + 4, 4) * 2 + core

    def remote(src, dst, send, recv, seq_id, head_id):
        return pltpu.make_async_remote_copy(
            src_ref=src, dst_ref=dst, send_sem=send, recv_sem=recv,
            device_id={"seq": seq_id, "head": head_id}, device_id_type=MESH,
        )

    barrier = pltpu.get_barrier_semaphore()
    for da, db in ((1, 0), (-1, 0), (0, 1), (0, -1)):
        pl.semaphore_signal(barrier, inc=1, device_id={"seq": slot(da, db), "head": h}, device_id_type=MESH)
    for d in range(1, 8):
        pl.semaphore_signal(barrier, inc=1, device_id={"seq": s, "head": lax.rem(h + d, 8)}, device_id_type=MESH)
    pl.semaphore_wait(barrier, 11)

    turns = (0, -1, 1, 2)

    class Gather:
        def __init__(self, mine, whole, first, second, send, recv):
            self.mine, self.whole, self.first, self.second = mine, whole, first, second
            self.send, self.recv = send, recv

        def copy(self, m, src, dst, da, db):
            return remote(src, dst, self.send.at[m], self.recv.at[m], slot(da, db), h)

        def start_own(self):
            me = self.whole(slot(0, 0))
            self.copy(0, self.mine, me, 1, 0).start()
            self.copy(1, self.mine, me, -1, 0).start()
            self.copy(4, self.mine, me, 0, 1).start()
            self.copy(5, self.mine, me, 0, -1).start()

        def got(self, m, region):
            self.copy(m, region, region, 1, 0).wait_recv()

        def forward_b(self, q):
            region = self.whole(slot(turns[q], 0))
            self.copy(4 + 2 * q, region, region, 0, 1).start()
            self.copy(5 + 2 * q, region, region, 0, -1).start()

        def second_step(self):
            self.got(0, self.whole(slot(-1, 0)))
            self.got(1, self.whole(slot(1, 0)))
            ra, rb = self.first(slot(-1, 0)), self.second(slot(1, 0))
            self.copy(2, ra, ra, 1, 0).start()
            self.copy(3, rb, rb, -1, 0).start()
            self.forward_b(1)
            self.forward_b(2)

        def third_step(self):
            self.got(2, self.first(slot(2, 0)))
            self.got(3, self.second(slot(2, 0)))
            self.forward_b(3)

        def fourth_step(self):
            for q in range(4):
                self.got(4 + 2 * q, self.whole(slot(turns[q], -1)))
                self.got(5 + 2 * q, self.whole(slot(turns[q], 1)))
                ra, rb = self.first(slot(turns[q], -1)), self.second(slot(turns[q], 1))
                self.copy(12 + 2 * q, ra, ra, 0, 1).start()
                self.copy(13 + 2 * q, rb, rb, 0, -1).start()

        def last_step(self):
            for q in range(4):
                self.got(12 + 2 * q, self.first(slot(turns[q], 2)))
                self.got(13 + 2 * q, self.second(slot(turns[q], 2)))

        def drain(self):
            me = self.mine
            for m in (0, 1, 4, 5):
                self.copy(m, me, me, 1, 0).wait_send()
            for m in (2, 12, 14, 16, 18):
                r = self.first(slot(0, 0))
                self.copy(m, r, r, 1, 0).wait_send()
            for m in (3, 13, 15, 17, 19):
                r = self.second(slot(0, 0))
                self.copy(m, r, r, 1, 0).wait_send()
            for m in (6, 7, 8, 9, 10, 11):
                r = self.whole(slot(0, 0))
                self.copy(m, r, r, 1, 0).wait_send()

    def wq_rows(offset, count):
        return lambda sl: wq.at[pl.ds(pl.multiple_of(sl * piece + offset, 16), count)]

    gather_q = Gather(w_mine, wq_rows(0, piece), wq_rows(0, piece // 2), wq_rows(piece // 2, piece // 2), w_send, w_recv)

    def wo_part(core, lo, count):
        return lambda sl: wo.at[
            pl.ds(pl.multiple_of(sl * piece + core * half_o, 16), half_o), pl.ds(lo, count)
        ]

    gather_o = Gather(
        wo_mine.at[pl.ds(pl.multiple_of(c * half_o, 16), half_o)],
        wo_part(c, 0, width), wo_part(c, 0, width // 2), wo_part(c, width // 2, width // 2), o_send, o_recv,
    )

    def partner_copy(sl, core):
        region = wo_part(core, 0, width)(sl)
        return remote(region, region, p_send.at[sl], p_recv.at[sl], s, head_of(0, 1 - c))

    gather_q.start_own()

    def row_block(dy, core, offset=0, count=own):
        return rows.at[lax.rem(y + dy + 4, 4), pl.ds(pl.multiple_of(core * own + offset, 16), count)]

    def norm_rows(i, carry):
        values = hidden[pl.ds(pl.multiple_of(i * 32, 32), 32), :].astype(F32)
        meansq = jnp.mean(values * values, axis=-1, keepdims=True)
        normed = (values * lax.rsqrt(meansq + 1e-05) * gain[...]).astype(BF16)
        rows[y, pl.ds(pl.multiple_of(c * own + i * 32, 32), 32), :] = normed
        return carry

    lax.fori_loop(0, own // 32, norm_rows, 0)

    def y_copy(m, region, dy, core):
        return remote(region, region, y_send.at[m], y_recv.at[m], s, head_of(dy, core))

    y_copy(1, row_block(0, c), 1, c).start()
    y_copy(2, row_block(0, c), -1, c).start()
    y_copy(0, row_block(0, c), 0, 1 - c).start()

    wq[pl.ds(pl.multiple_of(s * piece, 16), piece), :] = w_mine[...]
    wo[pl.ds(pl.multiple_of(s * piece, 16), piece), :] = wo_mine[...]

    def prepare_cache(i, carry):
        at = pl.ds(pl.multiple_of(i * 256, 256), 256)
        block = kv[at, :].astype(F32)
        low = block[:, :128]
        lane = lax.broadcasted_iota(jnp.int32, (256, 128), 1)
        position = i * 256 + lax.broadcasted_iota(jnp.int32, (256, 128), 0)
        hidden_slot = (lane == HEAD_DIM) & (position < WINDOW - prefix)
        key = jnp.where(lane < HEAD_DIM, low, 0.0)
        keys[at, :128] = jnp.where(hidden_slot, HIDE, key).astype(BF16)
        keys[at, 128:] = key.astype(BF16)
        vals[:HEAD_DIM, at] = jnp.transpose(block)[HEAD_DIM:, :].astype(BF16)
        return carry

    lax.fori_loop(0, WINDOW // 256, prepare_cache, 0)
    total = vals.shape[1]
    one_row = (lax.broadcasted_iota(jnp.int32, (16, 512), 0) == 0).astype(F32).astype(BF16)
    for i in range(total // 512):
        vals[HEAD_DIM:, i * 512 : (i + 1) * 512] = one_row
    for k in range(4):
        for i in range(3):
            cols = slice(i * 512, (i + 1) * 512)
            queries[k, 80:96, cols] = one_row
            queries[k, 96:128, cols] = jnp.zeros((32, 512), BF16)
            queries[k, 208:256, cols] = jnp.zeros((48, 512), BF16)

    gather_q.second_step()
    gather_q.third_step()
    gather_q.fourth_step()
    gather_o.start_own()
    y_copy(0, row_block(0, 1 - c), 0, c).wait_recv()
    gather_q.last_step()

    scale = math.log2(math.e) / math.sqrt(HEAD_DIM)

    def project(yk):
        projected = jnp.transpose(matmul(rows[yk], wq[...]))
        tokens = pl.ds(pl.multiple_of(yk * chip, 128), chip)
        cn, sn = cos_slot[:, tokens], sin_slot[:, tokens]
        cp, sp = cos_pre[:, 0:1], sin_pre[:, 0:1]
        cosine, sine = cn * cp - sn * sp, sn * cp + cn * sp

        def rotate(at):
            lead, trail = projected[at : at + HALF], projected[at + HALF : at + HEAD_DIM]
            turned = jnp.concatenate([lead * cosine - trail * sine, trail * cosine + lead * sine], axis=0)
            return turned.astype(BF16).astype(F32)

        for g in range(GROUP):
            scaled = rotate(g * HEAD_DIM) * scale
            high = scaled.astype(BF16)
            low = (scaled - high.astype(F32)).astype(BF16)
            for j in range(3):
                cols = slice(j * 512 + g * 128, j * 512 + g * 128 + 128)
                toks = slice(j * 128, j * 128 + 128)
                queries[yk, 0:80, cols] = high[:, toks]
                queries[yk, 128:208, cols] = low[:, toks]
        key = rotate(GROUP * HEAD_DIM)
        value = projected[(GROUP + 1) * HEAD_DIM : (GROUP + 2) * HEAD_DIM].astype(BF16)
        slots = pl.ds(pl.multiple_of(WINDOW + yk * chip, 128), chip)
        vals[:HEAD_DIM, slots] = value
        pair = jnp.transpose(jnp.concatenate([key, value.astype(F32)], axis=0))
        index = yk * chip + lax.broadcasted_iota(jnp.int32, pair.shape, 0)
        written[tokens, :] = jnp.where(index < length, pair, 0.0).astype(BF16)
        lane = lax.broadcasted_iota(jnp.int32, (chip, 128), 1)
        clean = jnp.where(lane < HEAD_DIM, pair[:, :128], 0.0).astype(BF16)
        keys[slots, :128] = clean
        keys[slots, 128:] = clean

    def scores(start, count, block_queries):
        return matmul(keys[pl.ds(pl.multiple_of(start, 128), count), :], block_queries)

    def absorb(carry, sc, parts):
        peak, total_ = carry
        top = jnp.max(sc, axis=0, keepdims=True)
        if peak is not None:
            top = jnp.maximum(peak, top)
        weights = jnp.exp2(sc - top).astype(BF16)
        if peak is not None:
            total_ = total_ * jnp.exp2(peak - top)
        at = 0
        for start, count in parts:
            add = matmul(vals[:88, pl.ds(pl.multiple_of(start, 128), count)], weights[at : at + count])
            total_ = add if total_ is None else total_ + add
            at += count
        return top, total_

    common = 4 * chip
    chunk1 = 512

    def first_phase(yk):
        todo = [(j, common + i * chunk1) for j in range(3) for i in range((WINDOW - common) // chunk1)]
        per = len(todo) // 3

        def make(t):
            j, start = todo[t]
            return scores(start, chunk1, queries[yk, :, j * 512 : (j + 1) * 512])

        sc = make(0)
        carry = (None, None)
        for t in range(len(todo)):
            later = make(t + 1) if t + 1 < len(todo) else None
            j, start = todo[t]
            carry = absorb(carry, sc, [(start, chunk1)])
            if t % per == per - 1:
                cols = slice(j * 512, (j + 1) * 512)
                maxes[yk, :, cols] = carry[0]
                state[yk, :, cols] = carry[1]
                carry = (None, None)
            sc = later

    def second_phase(yk):
        base = yk * chip
        full = [
            jnp.where(yk + i < 3, base + (i + 1) * chip, WINDOW + (i - (3 - yk)) * chip) for i in range(3)
        ]

        def make(j, u):
            block_queries = queries[yk, :, j * 512 : (j + 1) * 512]
            if u < 3:
                return scores(full[u], chip, block_queries)
            lowest, upto = chip - j * 128, (j + 1) * 128
            row = lax.broadcasted_iota(jnp.int32, (128, 512), 0)
            col = lax.broadcasted_iota(jnp.int32, (128, 512), 1) & (QBLOCK - 1)
            low = scores(base + j * 128, lowest, block_queries)
            high = scores(WINDOW + base, upto, block_queries)
            parts = [jnp.where(row > col, low[:128], HIDE), low[128:], high[:-128], jnp.where(row <= col, high[-128:], HIDE)]
            return jnp.concatenate([p for p in parts if p.shape[0]], axis=0)

        units = [(j, u) for j in range(3) for u in range(4)]
        sc = make(*units[0])
        for t, (j, u) in enumerate(units):
            later = make(*units[t + 1]) if t + 1 < len(units) else None
            cols = slice(j * 512, (j + 1) * 512)
            if u == 0:
                carry = (maxes[yk, :, cols], state[yk, :, cols])
            if u < 3:
                parts = [(full[u], chip)]
            else:
                parts = [(base + j * 128, chip - j * 128), (WINDOW + base, (j + 1) * 128)]
            carry = absorb(carry, sc, parts)
            if u == 3:
                sums = carry[1]
                attended = sums[:HEAD_DIM] * (1.0 / sums[HEAD_DIM : HEAD_DIM + 1])
                token = base + j * 128 + (lax.broadcasted_iota(jnp.int32, (HEAD_DIM, 512), 1) & (QBLOCK - 1))
                attended = jnp.where(token < length, attended, 0.0).astype(BF16)
                for g in range(GROUP):
                    ready[yk, g * HEAD_DIM : (g + 1) * HEAD_DIM, j * 128 : (j + 1) * 128] = attended[:, g * 128 : (g + 1) * 128]
            sc = later

    def arrive(k):
        @pl.when(k == 1)
        def _():
            y_copy(1, row_block(-1, c), 0, c).wait_recv()
            y_copy(2, row_block(1, c), 0, c).wait_recv()
            r = row_block(-1, c, 0, own // 2)
            y_copy(5, r, 1, c).start()
            r = row_block(1, c, own // 2, own // 2)
            y_copy(6, r, -1, c).start()
            y_copy(3, row_block(-1, c), 0, 1 - c).start()
            y_copy(4, row_block(1, c), 0, 1 - c).start()
            gather_o.second_step()
            y_copy(3, row_block(-1, 1 - c), 0, c).wait_recv()

        @pl.when(k == 2)
        def _():
            gather_o.third_step()
            y_copy(4, row_block(1, 1 - c), 0, c).wait_recv()

        @pl.when(k == 3)
        def _():
            y_copy(5, row_block(2, c, 0, own // 2), 0, c).wait_recv()
            y_copy(6, row_block(2, c, own // 2, own // 2), 0, c).wait_recv()
            y_copy(7, row_block(2, c), 0, 1 - c).start()
            gather_o.fourth_step()
            for q in range(1, 4):
                partner_copy(slot(turns[q], 0), c).start()
            for q in range(4):
                partner_copy(slot(turns[q], -1), c).start()
                partner_copy(slot(turns[q], 1), c).start()
            y_copy(7, row_block(2, 1 - c), 0, c).wait_recv()

    def first_loop(k, carry):
        arrive(k)
        turn = jnp.where(k == 0, 0, jnp.where(k == 1, 3, k - 1))
        yk = lax.rem(y + turn, 4)
        project(yk)
        first_phase(yk)
        return carry

    lax.fori_loop(0, 4, first_loop, 0)

    def attended_copy(yk, core):
        src = ready.at[yk, :, pl.ds(pl.multiple_of(core * 128, 128), 256)]
        dst = landed.at[pl.ds(pl.multiple_of(h * GROUP * HEAD_DIM, 16), GROUP * HEAD_DIM)]
        return remote(src, dst, a_send.at[2 * yk + core], a_recv.at[h], s, 2 * yk + core)

    def second_loop(k, carry):
        turn = jnp.where(k == 0, 2, jnp.where(k == 1, 1, jnp.where(k == 2, 3, 0)))
        yk = lax.rem(y + turn, 4)

        @pl.when(k == 1)
        def _():
            gather_o.last_step()
            for q in range(4):
                partner_copy(slot(turns[q], 2), c).start()

        second_phase(yk)

        @pl.when(k < 3)
        def _():
            attended_copy(yk, 0).start()
            attended_copy(yk, 1).start()

        @pl.when(k == 3)
        def _():
            attended_copy(yk, 1 - c).start()

        return carry

    lax.fori_loop(0, 4, second_loop, 0)
    mine = pl.ds(pl.multiple_of(h * GROUP * HEAD_DIM, 16), GROUP * HEAD_DIM)
    landed[mine, :] = ready[y, :, pl.ds(pl.multiple_of(c * 128, 128), 256)]
    for d in range(1, 16):
        sl = lax.rem(s + d, 16)
        partner_copy(sl, 1 - c).wait_recv()
    for d in range(1, 8):
        src = lax.rem(h + d, 8)
        region = landed.at[pl.ds(pl.multiple_of(src * GROUP * HEAD_DIM, 16), GROUP * HEAD_DIM)]
        remote(region, region, a_send.at[0], a_recv.at[src], s, h).wait_recv()

    for i in range(width // 512):
        block = matmul(wo[i * 512 : (i + 1) * 512, :], landed[...])
        finished[:, i * 512 : (i + 1) * 512] = jnp.transpose(block)
    out[...] = finished[pl.ds(pl.multiple_of(c * (256 - own), 64), own), :].astype(BF16)

    gather_q.drain()
    gather_o.drain()
    for d in range(1, 16):
        partner_copy(lax.rem(s + d, 16), c).wait_send()
    for m in (0, 1, 2, 3, 4, 7):
        y_copy(m, row_block(0, c), 0, 1 - c).wait_send()
    for m in (5, 6):
        y_copy(m, row_block(0, c, 0, own // 2), 0, 1 - c).wait_send()
    for d in range(1, 8):
        dst = lax.rem(h + d, 8)
        region = landed.at[pl.ds(0, GROUP * HEAD_DIM)]
        remote(region, region, a_send.at[dst], a_recv.at[0], s, dst).wait_send()


def solution(mesh):
    def step(hidden, norm_gain, w_qkv, w_out, kv_cache, new_len, prefix_len):
        s, h = lax.axis_index("seq"), lax.axis_index("head")
        own, width = hidden.shape[1], hidden.shape[2]
        new_total = 8 * own
        wide = (GROUP + 2) * HEAD_DIM
        piece = w_qkv.shape[0]
        w_mine = lax.dynamic_slice(w_qkv, (0, h * wide), (piece, wide))
        wo_mine = w_out.T
        frequency = np.exp(np.arange(HALF, dtype=np.float64) * (-2.0 * math.log(10000.0) / HEAD_DIM))
        angles = frequency[:, None] * np.arange(new_total, dtype=np.float64)[None, :]
        cos_slot = jnp.asarray(np.cos(angles).astype(np.float32))
        sin_slot = jnp.asarray(np.sin(angles).astype(np.float32))
        prefix = lax.dynamic_index_in_dim(prefix_len, s, 0, keepdims=False).astype(F32)
        turn = prefix * jnp.asarray(frequency.astype(np.float32))
        cos_pre = jnp.broadcast_to(jnp.cos(turn)[:, None], (HALF, 128))
        sin_pre = jnp.broadcast_to(jnp.sin(turn)[:, None], (HALF, 128))
        chip = 2 * own
        dma = pltpu.SemaphoreType.DMA
        vmem = pl.BlockSpec(memory_space=pltpu.VMEM)
        smem = pl.BlockSpec(memory_space=pltpu.SMEM)
        attn_out, kv_written = pl.pallas_call(
            kernel,
            out_shape=(
                jax.ShapeDtypeStruct((own, width), BF16),
                jax.ShapeDtypeStruct((new_total, 2 * HEAD_DIM), BF16),
            ),
            in_specs=[vmem] * 9 + [smem] * 2,
            out_specs=(vmem, vmem),
            scratch_shapes=[
                pltpu.VMEM((4, chip, width), BF16),
                pltpu.VMEM((16 * piece, wide), BF16),
                pltpu.VMEM((16 * piece, width), BF16),
                pltpu.VMEM((WINDOW + new_total, 256), BF16),
                pltpu.VMEM((96, WINDOW + new_total), BF16),
                pltpu.VMEM((4, 256, 4 * chip), BF16),
                pltpu.VMEM((4, 88, 4 * chip), F32),
                pltpu.VMEM((4, 1, 4 * chip), F32),
                pltpu.VMEM((4, GROUP * HEAD_DIM, chip), BF16),
                pltpu.VMEM((8 * GROUP * HEAD_DIM, 256), BF16),
                pltpu.VMEM((256, width), F32),
                dma((20,)), dma((20,)), dma((20,)), dma((20,)), dma((16,)), dma((16,)),
                dma((8,)), dma((8,)), dma((8,)), dma((8,)),
            ],
            compiler_params=pltpu.CompilerParams(
                collective_id=0, has_side_effects=True, vmem_limit_bytes=62 * 1024 * 1024
            ),
        )(
            hidden.reshape(own, width), norm_gain.reshape(1, width), w_mine, wo_mine,
            kv_cache.reshape(WINDOW, 2 * HEAD_DIM), cos_slot, sin_slot, cos_pre, sin_pre, new_len, prefix_len,
        )
        return attn_out.reshape(1, own, width), kv_written.reshape(1, new_total, 2 * HEAD_DIM)

    return jax.shard_map(
        step,
        mesh=mesh,
        in_specs=(
            P("seq", "head", None), P(), P("seq", None), P(None, "seq"), P("seq", None, "head"), P(), P(),
        ),
        out_specs=(P("seq", "head", None), P("seq", None, "head")),
        check_vma=False,
    )
```

```python
import math

import jax
import jax.numpy as jnp
import numpy as np
from jax import lax
from jax.experimental import pallas as pl
from jax.experimental.pallas import tpu as pltpu
from jax.sharding import PartitionSpec as P

HEAD_DIM = 80
HALF = HEAD_DIM // 2
GROUP = 4
WINDOW = 4096
QBLOCK = 128
SPLITS = ((80, 80),)
HIDE = -(2.0**127)
F32 = jnp.float32
BF16 = jnp.bfloat16
MESH = pl.DeviceIdType.MESH


def matmul(a, b):
    return lax.dot_general(a, b, (((1,), (0,)), ((), ())), preferred_element_type=F32)


def kernel(
    hidden_hbm, gain, w_mine, wo_mine, kv_hbm, cos_hbm, sin_hbm, frequency, new_len, prefix_len,
    out, written,
    hidden, cos_slot, sin_slot, cached_keys,
    rows, wq, wo, keys, vals, queries, state, maxes, ready, received, landed, turned,
    local, w_send, w_recv, o_send, o_recv, p_send, p_recv, y_send, y_recv, a_send, a_recv,
):
    s = lax.axis_index("seq")
    h = lax.axis_index("head")
    y, c = h // 2, h % 2
    own = hidden.shape[0]
    chip = 2 * own
    width = hidden.shape[1]
    piece = w_mine.shape[0]
    half_o = piece // 2
    length, prefix = new_len[s], prefix_len[s]
    x, z = s // 4, s % 4
    a, b = x + c * (z - x), z + c * (x - z)
    step_a, step_b = 4 - 3 * c, 1 + 3 * c

    fetches = []

    def fetch(src, dst):
        copy = pltpu.make_async_copy(src, dst, local.at[len(fetches)])
        copy.start()
        fetches.append(copy)
        return copy

    got_hidden = fetch(hidden_hbm, hidden)
    got_wq = fetch(w_mine, wq.at[pl.ds(pl.multiple_of(s * piece, 16), piece)])
    got_keys = fetch(kv_hbm.at[pl.ds(0, HEAD_DIM)], cached_keys)
    got_vals = fetch(kv_hbm.at[pl.ds(HEAD_DIM, HEAD_DIM)], vals.at[pl.ds(0, HEAD_DIM), pl.ds(0, WINDOW)])
    got_wo = fetch(wo_mine, wo.at[pl.ds(pl.multiple_of(s * piece, 16), piece)])
    got_cos = fetch(cos_hbm, cos_slot)
    got_sin = fetch(sin_hbm, sin_slot)

    def slot(da, db):
        return lax.rem(a + da + 4, 4) * step_a + lax.rem(b + db + 4, 4) * step_b

    def head_of(dy, core):
        return lax.rem(y + dy + 4, 4) * 2 + core

    def remote(src, dst, send, recv, seq_id, head_id):
        return pltpu.make_async_remote_copy(
            src_ref=src, dst_ref=dst, send_sem=send, recv_sem=recv,
            device_id={"seq": seq_id, "head": head_id}, device_id_type=MESH,
        )

    barrier = pltpu.get_barrier_semaphore()
    for da, db in ((1, 0), (-1, 0), (0, 1), (0, -1)):
        pl.semaphore_signal(barrier, inc=1, device_id={"seq": slot(da, db), "head": h}, device_id_type=MESH)
    for d in range(1, 8):
        pl.semaphore_signal(barrier, inc=1, device_id={"seq": s, "head": lax.rem(h + d, 8)}, device_id_type=MESH)
    pl.semaphore_wait(barrier, 11)

    turns = (0, -1, 1, 2)

    class Gather:
        def __init__(self, mine, whole, first, second, send, recv, at=0):
            self.mine, self.whole, self.first, self.second = mine, whole, first, second
            self.send, self.recv, self.at = send, recv, at

        def copy(self, m, src, dst, da, db):
            return remote(src, dst, self.send.at[self.at + m], self.recv.at[self.at + m], slot(da, db), h)

        def start_a(self):
            me = self.whole(slot(0, 0))
            self.copy(0, self.mine, me, 1, 0).start()
            self.copy(1, self.mine, me, -1, 0).start()

        def start_b(self):
            me = self.whole(slot(0, 0))
            self.copy(4, self.mine, me, 0, 1).start()
            self.copy(5, self.mine, me, 0, -1).start()

        def got(self, m, region):
            self.copy(m, region, region, 1, 0).wait_recv()

        def forward_b(self, q):
            region = self.whole(slot(turns[q], 0))
            self.copy(4 + 2 * q, region, region, 0, 1).start()
            self.copy(5 + 2 * q, region, region, 0, -1).start()

        def second_step(self):
            self.got(0, self.whole(slot(-1, 0)))
            self.got(1, self.whole(slot(1, 0)))
            ra, rb = self.first(slot(-1, 0)), self.second(slot(1, 0))
            self.copy(2, ra, ra, 1, 0).start()
            self.copy(3, rb, rb, -1, 0).start()
            self.forward_b(1)
            self.forward_b(2)

        def third_step(self):
            self.got(2, self.first(slot(2, 0)))
            self.got(3, self.second(slot(2, 0)))
            self.forward_b(3)

        def fourth_step(self, shards):
            for q in shards:
                self.got(4 + 2 * q, self.whole(slot(turns[q], -1)))
                self.got(5 + 2 * q, self.whole(slot(turns[q], 1)))
                ra, rb = self.first(slot(turns[q], -1)), self.second(slot(turns[q], 1))
                self.copy(12 + 2 * q, ra, ra, 0, 1).start()
                self.copy(13 + 2 * q, rb, rb, 0, -1).start()

        def last_step(self):
            for q in range(4):
                self.got(12 + 2 * q, self.first(slot(turns[q], 2)))
                self.got(13 + 2 * q, self.second(slot(turns[q], 2)))

        def drain(self):
            me = self.mine
            for m in (0, 1, 4, 5):
                self.copy(m, me, me, 1, 0).wait_send()
            for m in (2, 12, 14, 16, 18):
                r = self.first(slot(0, 0))
                self.copy(m, r, r, 1, 0).wait_send()
            for m in (3, 13, 15, 17, 19):
                r = self.second(slot(0, 0))
                self.copy(m, r, r, 1, 0).wait_send()
            for m in (6, 7, 8, 9, 10, 11):
                r = self.whole(slot(0, 0))
                self.copy(m, r, r, 1, 0).wait_send()

    def wq_rows(offset, count):
        return lambda sl: wq.at[pl.ds(pl.multiple_of(sl * piece + offset, 16), count)]

    gathers_q, at = [], 0
    for i, (one, two) in enumerate(SPLITS):
        gathers_q.append(
            Gather(
                wq_rows(at, one + two)(s), wq_rows(at, one + two), wq_rows(at, one), wq_rows(at + one, two),
                w_send, w_recv, 20 * i,
            )
        )
        at += one + two

    def wo_part(core, lo, count):
        return lambda sl: wo.at[
            pl.ds(pl.multiple_of(sl * piece + core * half_o, 16), half_o), pl.ds(lo, count)
        ]

    gather_o = Gather(
        wo_mine.at[pl.ds(pl.multiple_of(c * half_o, 16), half_o)],
        wo_part(c, 0, width), wo_part(c, 0, width // 2), wo_part(c, width // 2, width // 2), o_send, o_recv,
    )

    def partner_copy(sl, core):
        region = wo_part(core, 0, width)(sl)
        return remote(region, region, p_send.at[sl], p_recv.at[sl], s, head_of(0, 1 - c))

    got_wq.wait()
    for gather_q in gathers_q:
        gather_q.start_a()
        gather_q.start_b()
    got_hidden.wait()

    def row_block(dy, core, offset=0, count=own):
        return rows.at[lax.rem(y + dy + 4, 4), pl.ds(pl.multiple_of(core * own + offset, 16), count)]

    def norm_rows(i, carry):
        values = hidden[pl.ds(pl.multiple_of(i * 32, 32), 32), :].astype(F32)
        meansq = jnp.mean(values * values, axis=-1, keepdims=True)
        normed = (values * lax.rsqrt(meansq + 1e-05) * gain[...].reshape(1, width)).astype(BF16)
        rows[y, pl.ds(pl.multiple_of(c * own + i * 32, 32), 32), :] = normed
        return carry

    lax.fori_loop(0, own // 32, norm_rows, 0)

    def y_copy(m, region, dy, core):
        return remote(region, region, y_send.at[m], y_recv.at[m], s, head_of(dy, core))

    half = own // 2
    y_copy(1, row_block(0, c, 0, half), 1, c).start()
    y_copy(3, row_block(0, c, half, half), -1, c).start()
    y_copy(2, row_block(0, c, half, half), 1, c).start()
    y_copy(4, row_block(0, c, 0, half), -1, c).start()
    y_copy(0, row_block(0, c), 0, 1 - c).start()

    for gather_q in gathers_q:
        gather_q.second_step()
    got_keys.wait()

    def prepare_cache(i, carry):
        at = pl.ds(pl.multiple_of(i * 256, 256), 256)
        token = i * 256 + lax.broadcasted_iota(jnp.int32, (48, 256), 1)
        first = lax.broadcasted_iota(jnp.int32, (48, 256), 0) == 0
        bias = jnp.where(first & (token < WINDOW - prefix), HIDE, 0.0)
        block = jnp.transpose(jnp.concatenate([cached_keys[:, at].astype(F32), bias], axis=0))
        lane = lax.broadcasted_iota(jnp.int32, (256, 128), 1)
        keys[at, :128] = block.astype(BF16)
        keys[at, 128:] = jnp.where(lane < HEAD_DIM, block, 0.0).astype(BF16)
        return carry

    lax.fori_loop(0, WINDOW // 256, prepare_cache, 0)
    for gather_q in gathers_q:
        gather_q.third_step()
    got_wo.wait()
    got_vals.wait()
    got_cos.wait()
    got_sin.wait()
    total = vals.shape[1]
    one_row = (lax.broadcasted_iota(jnp.int32, (16, 512), 0) == 0).astype(F32).astype(BF16)
    for i in range(total // 512):
        vals[HEAD_DIM:, i * 512 : (i + 1) * 512] = one_row
    for k in range(4):
        for i in range(3):
            cols = slice(i * 512, (i + 1) * 512)
            queries[k, 80:96, cols] = one_row
            queries[k, 96:128, cols] = jnp.zeros((32, 512), BF16)
            queries[k, 208:256, cols] = jnp.zeros((48, 512), BF16)
    turn_pre = frequency[...] * prefix.astype(F32)
    cp, sp = jnp.cos(turn_pre)[:, 0:1], jnp.sin(turn_pre)[:, 0:1]

    for gather_q in gathers_q:
        gather_q.fourth_step(range(4))
    gather_o.start_a()
    gather_o.start_b()
    y_copy(0, row_block(0, 1 - c), 0, c).wait_recv()
    y_copy(1, row_block(-1, c, 0, half), 0, c).wait_recv()
    y_copy(5, row_block(-1, c, 0, half), 1, c).start()
    y_copy(3, row_block(1, c, half, half), 0, c).wait_recv()
    y_copy(6, row_block(1, c, half, half), -1, c).start()
    y_copy(7, row_block(-1, c, 0, half), 0, 1 - c).start()
    y_copy(9, row_block(1, c, half, half), 0, 1 - c).start()
    for gather_q in gathers_q:
        gather_q.last_step()

    scale = math.log2(math.e) / math.sqrt(HEAD_DIM)

    def project(yk):
        projected = jnp.transpose(matmul(rows[yk], wq[...]))
        tokens = pl.ds(pl.multiple_of(yk * chip, 128), chip)
        cn, sn = cos_slot[:, tokens], sin_slot[:, tokens]
        cosine, sine = cn * cp - sn * sp, sn * cp + cn * sp

        def rotate(at):
            lead, trail = projected[at : at + HALF], projected[at + HALF : at + HEAD_DIM]
            turned = jnp.concatenate([lead * cosine - trail * sine, trail * cosine + lead * sine], axis=0)
            return turned.astype(BF16).astype(F32)

        for g in range(GROUP):
            scaled = rotate(g * HEAD_DIM) * scale
            high = scaled.astype(BF16)
            low = (scaled - high.astype(F32)).astype(BF16)
            for j in range(3):
                cols = slice(j * 512 + g * 128, j * 512 + g * 128 + 128)
                toks = slice(j * 128, j * 128 + 128)
                queries[yk, 0:80, cols] = high[:, toks]
                queries[yk, 128:208, cols] = low[:, toks]
        key = rotate(GROUP * HEAD_DIM)
        value = projected[(GROUP + 1) * HEAD_DIM : (GROUP + 2) * HEAD_DIM].astype(BF16)
        slots = pl.ds(pl.multiple_of(WINDOW + yk * chip, 128), chip)
        vals[:HEAD_DIM, slots] = value
        pair = jnp.concatenate([key, value.astype(F32)], axis=0)
        index = yk * chip + lax.broadcasted_iota(jnp.int32, pair.shape, 1)
        written[:, tokens] = jnp.where(index < length, pair, 0.0).astype(BF16)
        clean = jnp.transpose(jnp.concatenate([key, jnp.zeros((48, chip), F32)], axis=0)).astype(BF16)
        keys[slots, :128] = clean
        keys[slots, 128:] = clean

    def scores(start, count, block_queries):
        return matmul(keys[pl.ds(pl.multiple_of(start, 128), count), :], block_queries)

    def absorb(carry, sc, parts):
        peak, total_ = carry
        top = jnp.max(sc, axis=0, keepdims=True)
        if peak is not None:
            top = jnp.maximum(peak, top)
        weights = jnp.exp2(sc - top).astype(BF16)
        if peak is not None:
            total_ = total_ * jnp.exp2(peak - top)
        at = 0
        for start, count in parts:
            add = matmul(vals[:88, pl.ds(pl.multiple_of(start, 128), count)], weights[at : at + count])
            total_ = add if total_ is None else total_ + add
            at += count
        return top, total_

    common = 4 * chip
    chunk1 = 512

    def first_phase(yk):
        todo = [(j, common + i * chunk1) for j in range(3) for i in range((WINDOW - common) // chunk1)]
        per = len(todo) // 3

        def make(t):
            j, start = todo[t]
            return scores(start, chunk1, queries[yk, :, j * 512 : (j + 1) * 512])

        sc = make(0)
        carry = (None, None)
        for t in range(len(todo)):
            later = make(t + 1) if t + 1 < len(todo) else None
            j, start = todo[t]
            carry = absorb(carry, sc, [(start, chunk1)])
            if t % per == per - 1:
                cols = slice(j * 512, (j + 1) * 512)
                maxes[yk, :, cols] = carry[0]
                state[yk, :, cols] = carry[1]
                carry = (None, None)
            sc = later

    def second_phase(yk):
        base = yk * chip
        full = [
            jnp.where(yk + i < 3, base + (i + 1) * chip, WINDOW + (i - (3 - yk)) * chip) for i in range(3)
        ]

        def make(j, u):
            block_queries = queries[yk, :, j * 512 : (j + 1) * 512]
            if u < 3:
                return scores(full[u], chip, block_queries)
            lowest, upto = chip - j * 128, (j + 1) * 128
            row = lax.broadcasted_iota(jnp.int32, (128, 512), 0)
            col = lax.broadcasted_iota(jnp.int32, (128, 512), 1) & (QBLOCK - 1)
            low = scores(base + j * 128, lowest, block_queries)
            high = scores(WINDOW + base, upto, block_queries)
            parts = [jnp.where(row > col, low[:128], HIDE), low[128:], high[:-128], jnp.where(row <= col, high[-128:], HIDE)]
            return jnp.concatenate([p for p in parts if p.shape[0]], axis=0)

        units = [(j, u) for j in range(3) for u in range(4)]
        sc = make(*units[0])
        for t, (j, u) in enumerate(units):
            later = make(*units[t + 1]) if t + 1 < len(units) else None
            cols = slice(j * 512, (j + 1) * 512)
            if u == 0:
                carry = (maxes[yk, :, cols], state[yk, :, cols])
            if u < 3:
                parts = [(full[u], chip)]
            else:
                parts = [(base + j * 128, chip - j * 128), (WINDOW + base, (j + 1) * 128)]
            carry = absorb(carry, sc, parts)
            if u == 3:
                sums = carry[1]
                attended = sums[:HEAD_DIM] * (1.0 / sums[HEAD_DIM : HEAD_DIM + 1])
                token = base + j * 128 + (lax.broadcasted_iota(jnp.int32, (HEAD_DIM, 512), 1) & (QBLOCK - 1))
                attended = jnp.where(token < length, attended, 0.0)
                heads = [attended[:, g * 128 : (g + 1) * 128] for g in range(GROUP)]
                if j == 1:
                    left = lax.broadcasted_iota(jnp.int32, (HEAD_DIM, 128), 1) < 64
                    for p in range(2):
                        one, two = heads[p], heads[p + 2]
                        at = slice(320 + p * HEAD_DIM, 320 + (p + 1) * HEAD_DIM)
                        ready[yk, 0, at, :] = jnp.where(left, one, pltpu.roll(two, 64, 1)).astype(BF16)
                        ready[yk, 1, at, :] = jnp.where(left, pltpu.roll(one, 64, 1), two).astype(BF16)
                else:
                    for g in range(GROUP):
                        ready[yk, j // 2, g * HEAD_DIM : (g + 1) * HEAD_DIM, :] = heads[g].astype(BF16)
            sc = later

    def arrive(k):
        @pl.when(k == 1)
        def _():
            y_copy(2, row_block(-1, c, half, half), 0, c).wait_recv()
            y_copy(8, row_block(-1, c, half, half), 0, 1 - c).start()
            y_copy(4, row_block(1, c, 0, half), 0, c).wait_recv()
            y_copy(10, row_block(1, c, 0, half), 0, 1 - c).start()
            gather_o.second_step()
            y_copy(7, row_block(-1, 1 - c, 0, half), 0, c).wait_recv()
            y_copy(8, row_block(-1, 1 - c, half, half), 0, c).wait_recv()

        @pl.when(k == 2)
        def _():
            gather_o.third_step()
            y_copy(9, row_block(1, 1 - c, half, half), 0, c).wait_recv()
            y_copy(10, row_block(1, 1 - c, 0, half), 0, c).wait_recv()

        @pl.when(k == 3)
        def _():
            y_copy(5, row_block(2, c, 0, half), 0, c).wait_recv()
            y_copy(6, row_block(2, c, half, half), 0, c).wait_recv()
            y_copy(11, row_block(2, c), 0, 1 - c).start()
            gather_o.fourth_step((0, 1, 2))
            for q in range(1, 4):
                partner_copy(slot(turns[q], 0), c).start()
            y_copy(11, row_block(2, 1 - c), 0, c).wait_recv()

    def first_loop(k, carry):
        arrive(k)
        turn = jnp.where(k == 0, 0, jnp.where(k == 1, 3, k - 1))
        yk = lax.rem(y + turn, 4)
        project(yk)
        first_phase(yk)
        return carry

    lax.fori_loop(0, 4, first_loop, 0)

    def attended_copy(yk, core):
        return remote(
            ready.at[yk, core], received.at[h], a_send.at[2 * yk + core], a_recv.at[h], s, 2 * yk + core
        )

    def second_loop(k, carry):
        turn = jnp.where(k == 0, 2, jnp.where(k == 1, 1, jnp.where(k == 2, 3, 0)))
        yk = lax.rem(y + turn, 4)

        @pl.when(k == 0)
        def _():
            gather_o.fourth_step((3,))

        @pl.when(k == 1)
        def _():
            for q in range(4):
                partner_copy(slot(turns[q], -1), c).start()
                partner_copy(slot(turns[q], 1), c).start()

        @pl.when(k == 2)
        def _():
            gather_o.last_step()
            for q in range(4):
                partner_copy(slot(turns[q], 2), c).start()

        second_phase(yk)

        @pl.when(k < 3)
        def _():
            attended_copy(yk, 0).start()
            attended_copy(yk, 1).start()

        @pl.when(k == 3)
        def _():
            attended_copy(yk, 1 - c).start()

        return carry

    lax.fori_loop(0, 4, second_loop, 0)

    def unpack(src_head, block):
        top = src_head * GROUP * HEAD_DIM
        landed[pl.ds(pl.multiple_of(top, 16), GROUP * HEAD_DIM), :128] = block[: GROUP * HEAD_DIM]
        packed = block[GROUP * HEAD_DIM :]
        landed[pl.ds(pl.multiple_of(top, 16), 2 * HEAD_DIM), 128:] = packed
        turned_back = pltpu.roll(packed.astype(F32), 64, 1).astype(BF16)
        landed[pl.ds(pl.multiple_of(top + 2 * HEAD_DIM, 16), 2 * HEAD_DIM), 128:] = turned_back

    unpack(h, ready[y, c])
    for d in range(1, 16):
        sl = lax.rem(s + d, 16)
        partner_copy(sl, 1 - c).wait_recv()

    for dy, core in ((0, 1 - c), (2, 0), (2, 1), (1, 0), (1, 1), (-1, 0), (-1, 1)):
        src = head_of(dy, core)
        remote(received.at[src], received.at[src], a_send.at[0], a_recv.at[src], s, h).wait_recv()
        unpack(src, received[src])
    for i in range(width // 512):
        turned[:, i * 512 : (i + 1) * 512] = jnp.transpose(matmul(wo[i * 512 : (i + 1) * 512, :], landed[...]))
    rest = own - 128
    out[pl.ds(pl.multiple_of(c * rest, 64), 128), :] = turned[:128, :].astype(BF16)
    out[pl.ds(pl.multiple_of((1 - c) * 128, 64), rest), :] = turned[128:own, :].astype(BF16)

    for gather_q in gathers_q:
        gather_q.drain()
    gather_o.drain()
    for d in range(1, 16):
        partner_copy(lax.rem(s + d, 16), c).wait_send()
    for m in (0, 11):
        y_copy(m, row_block(0, c), 0, 1 - c).wait_send()
    for m in range(1, 11):
        y_copy(m, row_block(0, c, 0, half), 0, 1 - c).wait_send()
    for d in range(1, 8):
        dst = lax.rem(h + d, 8)
        remote(received.at[0], received.at[0], a_send.at[dst], a_recv.at[0], s, dst).wait_send()


def solution(mesh):
    def step(hidden, norm_gain, w_qkv, w_out, kv_cache, new_len, prefix_len):
        s, h = lax.axis_index("seq"), lax.axis_index("head")
        own, width = hidden.shape[1], hidden.shape[2]
        new_total = 8 * own
        wide = (GROUP + 2) * HEAD_DIM
        piece = w_qkv.shape[0]
        w_mine = lax.dynamic_slice(w_qkv, (0, h * wide), (piece, wide))
        wo_mine = w_out.T
        cached = jnp.swapaxes(kv_cache.reshape(WINDOW, 2 * HEAD_DIM), 0, 1)
        frequency = np.exp(np.arange(HALF, dtype=np.float64) * (-2.0 * math.log(10000.0) / HEAD_DIM))
        angles = frequency[:, None] * np.arange(new_total, dtype=np.float64)[None, :]
        cos_slot = jnp.asarray(np.cos(angles).astype(np.float32))
        sin_slot = jnp.asarray(np.sin(angles).astype(np.float32))
        lanes = jnp.asarray(np.broadcast_to(frequency[:, None], (HALF, 128)).astype(np.float32))
        chip = 2 * own
        dma = pltpu.SemaphoreType.DMA
        vmem = pl.BlockSpec(memory_space=pltpu.VMEM)
        smem = pl.BlockSpec(memory_space=pltpu.SMEM)
        any_ = pl.BlockSpec(memory_space=pl.ANY)
        attn_out, kv_written = pl.pallas_call(
            kernel,
            out_shape=(
                pltpu.VMEM((own, width), BF16),
                pltpu.VMEM((2 * HEAD_DIM, new_total), BF16),
            ),
            in_specs=[any_, vmem, any_, any_, any_, any_, any_, vmem, smem, smem],
            out_specs=(vmem, vmem),
            scratch_shapes=[
                pltpu.VMEM((own, width), BF16),
                pltpu.VMEM((HALF, new_total), F32),
                pltpu.VMEM((HALF, new_total), F32),
                pltpu.VMEM((HEAD_DIM, WINDOW), BF16),
                pltpu.VMEM((4, chip, width), BF16),
                pltpu.VMEM((16 * piece, wide), BF16),
                pltpu.VMEM((16 * piece, width), BF16),
                pltpu.VMEM((WINDOW + new_total, 256), BF16),
                pltpu.VMEM((96, WINDOW + new_total), BF16),
                pltpu.VMEM((4, 256, 4 * chip), BF16),
                pltpu.VMEM((4, 88, 4 * chip), F32),
                pltpu.VMEM((4, 1, 4 * chip), F32),
                pltpu.VMEM((4, 2, 6 * HEAD_DIM, 128), BF16),
                pltpu.VMEM((8, 6 * HEAD_DIM, 128), BF16),
                pltpu.VMEM((8 * GROUP * HEAD_DIM, 256), BF16),
                pltpu.VMEM((256, width), F32),
                dma((7,)), dma((20 * len(SPLITS),)), dma((20 * len(SPLITS),)), dma((20,)), dma((20,)), dma((16,)), dma((16,)),
                dma((12,)), dma((12,)), dma((8,)), dma((8,)),
            ],
            compiler_params=pltpu.CompilerParams(
                collective_id=0, has_side_effects=True, vmem_limit_bytes=56 * 1024 * 1024
            ),
        )(
            hidden.reshape(own, width), norm_gain, w_mine, wo_mine,
            cached, cos_slot, sin_slot, lanes, new_len, prefix_len,
        )
        return attn_out.reshape(1, own, width), jnp.swapaxes(kv_written, 0, 1).reshape(1, new_total, 2 * HEAD_DIM)

    return jax.shard_map(
        step,
        mesh=mesh,
        in_specs=(
            P("seq", "head", None), P(), P("seq", None), P(None, "seq"), P("seq", None, "head"), P(), P(),
        ),
        out_specs=(P("seq", "head", None), P("seq", None, "head")),
        check_vma=False,
    )
```

```python
import math

import jax
import jax.numpy as jnp
import numpy as np
from jax import lax
from jax.experimental import pallas as pl
from jax.experimental.pallas import tpu as pltpu
from jax.sharding import PartitionSpec as P

HEAD_DIM = 80
HALF = HEAD_DIM // 2
GROUP = 4
WINDOW = 4096
QBLOCK = 128
SPLITS = ((80, 80),)
HIDE = -(2.0**127)
F32 = jnp.float32
BF16 = jnp.bfloat16
MESH = pl.DeviceIdType.MESH


def matmul(a, b):
    return lax.dot_general(a, b, (((1,), (0,)), ((), ())), preferred_element_type=F32)


def kernel(
    hidden_hbm, gain, w_mine, wo_mine, kv_hbm, cos_hbm, sin_hbm, frequency, new_len, prefix_len,
    out, written,
    hidden, cos_slot, sin_slot, cached_keys,
    rows, wq, wo, keys, vals, queries, state, maxes, ready, received, landed, turned,
    local, w_send, w_recv, o_send, o_recv, p_send, p_recv, y_send, y_recv, a_send, a_recv,
):
    s = lax.axis_index("seq")
    h = lax.axis_index("head")
    y, c = h // 2, h % 2
    own = hidden.shape[0]
    chip = 2 * own
    width = hidden.shape[1]
    piece = w_mine.shape[0]
    half_o = piece // 2
    length, prefix = new_len[s], prefix_len[s]
    x, z = s // 4, s % 4
    a, b = x + c * (z - x), z + c * (x - z)
    step_a, step_b = 4 - 3 * c, 1 + 3 * c

    fetches = []

    def fetch(src, dst):
        copy = pltpu.make_async_copy(src, dst, local.at[len(fetches)])
        copy.start()
        fetches.append(copy)
        return copy

    got_hidden = fetch(hidden_hbm, hidden)
    got_wq = fetch(w_mine, wq.at[pl.ds(pl.multiple_of(s * piece, 16), piece)])
    got_keys = fetch(kv_hbm.at[pl.ds(0, HEAD_DIM)], cached_keys)
    got_vals = fetch(kv_hbm.at[pl.ds(HEAD_DIM, HEAD_DIM)], vals.at[pl.ds(0, HEAD_DIM), pl.ds(0, WINDOW)])
    got_wo = fetch(wo_mine, wo.at[pl.ds(pl.multiple_of(s * piece, 16), piece)])
    got_cos = fetch(cos_hbm, cos_slot)
    got_sin = fetch(sin_hbm, sin_slot)

    def slot(da, db):
        return lax.rem(a + da + 4, 4) * step_a + lax.rem(b + db + 4, 4) * step_b

    def head_of(dy, core):
        return lax.rem(y + dy + 4, 4) * 2 + core

    def remote(src, dst, send, recv, seq_id, head_id):
        return pltpu.make_async_remote_copy(
            src_ref=src, dst_ref=dst, send_sem=send, recv_sem=recv,
            device_id={"seq": seq_id, "head": head_id}, device_id_type=MESH,
        )

    barrier = pltpu.get_barrier_semaphore()
    for da, db in ((1, 0), (-1, 0), (2, 0), (0, 1), (0, -1)):
        pl.semaphore_signal(barrier, inc=1, device_id={"seq": slot(da, db), "head": h}, device_id_type=MESH)
    for d in range(1, 8):
        pl.semaphore_signal(barrier, inc=1, device_id={"seq": s, "head": lax.rem(h + d, 8)}, device_id_type=MESH)
    pl.semaphore_wait(barrier, 12)

    turns = (0, -1, 1, 2)

    class Gather:
        def __init__(self, mine, whole, first, second, send, recv, at=0, direct=False):
            self.mine, self.whole, self.first, self.second = mine, whole, first, second
            self.send, self.recv, self.at, self.direct = send, recv, at, direct

        def copy(self, m, src, dst, da, db):
            return remote(src, dst, self.send.at[self.at + m], self.recv.at[self.at + m], slot(da, db), h)

        def start_a(self):
            me = self.whole(slot(0, 0))
            self.copy(0, self.mine, me, 1, 0).start()
            self.copy(1, self.mine, me, -1, 0).start()
            if self.direct:
                self.copy(2, self.mine, me, 2, 0).start()

        def start_b(self):
            me = self.whole(slot(0, 0))
            self.copy(4, self.mine, me, 0, 1).start()
            self.copy(5, self.mine, me, 0, -1).start()

        def got(self, m, region):
            self.copy(m, region, region, 1, 0).wait_recv()

        def forward_b(self, q):
            region = self.whole(slot(turns[q], 0))
            self.copy(4 + 2 * q, region, region, 0, 1).start()
            self.copy(5 + 2 * q, region, region, 0, -1).start()

        def second_step(self):
            self.got(0, self.whole(slot(-1, 0)))
            self.got(1, self.whole(slot(1, 0)))
            if not self.direct:
                ra, rb = self.first(slot(-1, 0)), self.second(slot(1, 0))
                self.copy(2, ra, ra, 1, 0).start()
                self.copy(3, rb, rb, -1, 0).start()
            self.forward_b(1)
            self.forward_b(2)

        def third_step(self):
            if self.direct:
                self.got(2, self.whole(slot(2, 0)))
            else:
                self.got(2, self.first(slot(2, 0)))
                self.got(3, self.second(slot(2, 0)))
            self.forward_b(3)

        def fourth_step(self, shards):
            for q in shards:
                self.got(4 + 2 * q, self.whole(slot(turns[q], -1)))
                self.got(5 + 2 * q, self.whole(slot(turns[q], 1)))
                ra, rb = self.first(slot(turns[q], -1)), self.second(slot(turns[q], 1))
                self.copy(12 + 2 * q, ra, ra, 0, 1).start()
                self.copy(13 + 2 * q, rb, rb, 0, -1).start()

        def last_step(self):
            for q in range(4):
                self.got(12 + 2 * q, self.first(slot(turns[q], 2)))
                self.got(13 + 2 * q, self.second(slot(turns[q], 2)))

        def drain(self):
            me = self.mine
            for m in (0, 1, 2, 4, 5) if self.direct else (0, 1, 4, 5):
                self.copy(m, me, me, 1, 0).wait_send()
            for m in (12, 14, 16, 18) if self.direct else (2, 12, 14, 16, 18):
                r = self.first(slot(0, 0))
                self.copy(m, r, r, 1, 0).wait_send()
            for m in (13, 15, 17, 19) if self.direct else (3, 13, 15, 17, 19):
                r = self.second(slot(0, 0))
                self.copy(m, r, r, 1, 0).wait_send()
            for m in (6, 7, 8, 9, 10, 11):
                r = self.whole(slot(0, 0))
                self.copy(m, r, r, 1, 0).wait_send()

    def wq_rows(offset, count):
        return lambda sl: wq.at[pl.ds(pl.multiple_of(sl * piece + offset, 16), count)]

    gathers_q, at = [], 0
    for i, (one, two) in enumerate(SPLITS):
        gathers_q.append(
            Gather(
                wq_rows(at, one + two)(s), wq_rows(at, one + two), wq_rows(at, one), wq_rows(at + one, two),
                w_send, w_recv, 20 * i, direct=True,
            )
        )
        at += one + two

    def wo_part(core, lo, count):
        return lambda sl: wo.at[
            pl.ds(pl.multiple_of(sl * piece + core * half_o, 16), half_o), pl.ds(lo, count)
        ]

    gather_o = Gather(
        wo_mine.at[pl.ds(pl.multiple_of(c * half_o, 16), half_o)],
        wo_part(c, 0, width), wo_part(c, 0, width // 2), wo_part(c, width // 2, width // 2), o_send, o_recv,
    )

    def partner_copy(sl, core):
        region = wo_part(core, 0, width)(sl)
        return remote(region, region, p_send.at[sl], p_recv.at[sl], s, head_of(0, 1 - c))

    got_wq.wait()
    for gather_q in gathers_q:
        gather_q.start_a()
        gather_q.start_b()
    got_hidden.wait()

    def row_block(dy, core, offset=0, count=own):
        return rows.at[lax.rem(y + dy + 4, 4), pl.ds(pl.multiple_of(core * own + offset, 16), count)]

    def norm_rows(i, carry):
        values = hidden[pl.ds(pl.multiple_of(i * 32, 32), 32), :].astype(F32)
        meansq = jnp.mean(values * values, axis=-1, keepdims=True)
        normed = (values * lax.rsqrt(meansq + 1e-05) * gain[...].reshape(1, width)).astype(BF16)
        rows[y, pl.ds(pl.multiple_of(c * own + i * 32, 32), 32), :] = normed
        return carry

    lax.fori_loop(0, own // 32, norm_rows, 0)

    def y_copy(m, region, dy, core):
        return remote(region, region, y_send.at[m], y_recv.at[m], s, head_of(dy, core))

    half = own // 2
    y_copy(1, row_block(0, c, 0, half), 1, c).start()
    y_copy(3, row_block(0, c, half, half), -1, c).start()
    y_copy(2, row_block(0, c, half, half), 1, c).start()
    y_copy(4, row_block(0, c, 0, half), -1, c).start()
    y_copy(0, row_block(0, c), 0, 1 - c).start()

    for gather_q in gathers_q:
        gather_q.second_step()
    got_keys.wait()

    def prepare_cache(i, carry):
        at = pl.ds(pl.multiple_of(i * 256, 256), 256)
        token = i * 256 + lax.broadcasted_iota(jnp.int32, (48, 256), 1)
        first = lax.broadcasted_iota(jnp.int32, (48, 256), 0) == 0
        bias = jnp.where(first & (token < WINDOW - prefix), HIDE, 0.0)
        block = jnp.transpose(jnp.concatenate([cached_keys[:, at].astype(F32), bias], axis=0))
        lane = lax.broadcasted_iota(jnp.int32, (256, 128), 1)
        keys[at, :128] = block.astype(BF16)
        keys[at, 128:] = jnp.where(lane < HEAD_DIM, block, 0.0).astype(BF16)
        return carry

    lax.fori_loop(0, WINDOW // 256, prepare_cache, 0)
    for gather_q in gathers_q:
        gather_q.third_step()
    got_wo.wait()
    got_vals.wait()
    got_cos.wait()
    got_sin.wait()
    total = vals.shape[1]
    one_row = (lax.broadcasted_iota(jnp.int32, (16, 512), 0) == 0).astype(F32).astype(BF16)
    for i in range(total // 512):
        vals[HEAD_DIM:, i * 512 : (i + 1) * 512] = one_row
    for k in range(4):
        for i in range(3):
            cols = slice(i * 512, (i + 1) * 512)
            queries[k, 80:96, cols] = one_row
            queries[k, 96:128, cols] = jnp.zeros((32, 512), BF16)
            queries[k, 208:256, cols] = jnp.zeros((48, 512), BF16)
    turn_pre = frequency[...] * prefix.astype(F32)
    cp, sp = jnp.cos(turn_pre)[:, 0:1], jnp.sin(turn_pre)[:, 0:1]

    for gather_q in gathers_q:
        gather_q.fourth_step(range(4))
    gather_o.start_a()
    y_copy(0, row_block(0, 1 - c), 0, c).wait_recv()
    y_copy(1, row_block(-1, c, 0, half), 0, c).wait_recv()
    y_copy(5, row_block(-1, c, 0, half), 1, c).start()
    y_copy(3, row_block(1, c, half, half), 0, c).wait_recv()
    y_copy(6, row_block(1, c, half, half), -1, c).start()
    y_copy(7, row_block(-1, c, 0, half), 0, 1 - c).start()
    y_copy(9, row_block(1, c, half, half), 0, 1 - c).start()
    for gather_q in gathers_q:
        gather_q.last_step()
    gather_o.start_b()

    scale = math.log2(math.e) / math.sqrt(HEAD_DIM)

    def project(yk):
        projected = jnp.transpose(matmul(rows[yk], wq[...]))
        tokens = pl.ds(pl.multiple_of(yk * chip, 128), chip)
        cn, sn = cos_slot[:, tokens], sin_slot[:, tokens]
        cosine, sine = cn * cp - sn * sp, sn * cp + cn * sp

        def rotate(at):
            lead, trail = projected[at : at + HALF], projected[at + HALF : at + HEAD_DIM]
            turned = jnp.concatenate([lead * cosine - trail * sine, trail * cosine + lead * sine], axis=0)
            return turned.astype(BF16).astype(F32)

        for g in range(GROUP):
            scaled = rotate(g * HEAD_DIM) * scale
            high = scaled.astype(BF16)
            low = (scaled - high.astype(F32)).astype(BF16)
            for j in range(3):
                cols = slice(j * 512 + g * 128, j * 512 + g * 128 + 128)
                toks = slice(j * 128, j * 128 + 128)
                queries[yk, 0:80, cols] = high[:, toks]
                queries[yk, 128:208, cols] = low[:, toks]
        key = rotate(GROUP * HEAD_DIM)
        value = projected[(GROUP + 1) * HEAD_DIM : (GROUP + 2) * HEAD_DIM].astype(BF16)
        slots = pl.ds(pl.multiple_of(WINDOW + yk * chip, 128), chip)
        vals[:HEAD_DIM, slots] = value
        pair = jnp.concatenate([key, value.astype(F32)], axis=0)
        index = yk * chip + lax.broadcasted_iota(jnp.int32, pair.shape, 1)
        written[:, tokens] = jnp.where(index < length, pair, 0.0).astype(BF16)
        clean = jnp.transpose(jnp.concatenate([key, jnp.zeros((48, chip), F32)], axis=0)).astype(BF16)
        keys[slots, :128] = clean
        keys[slots, 128:] = clean

    def scores(start, count, block_queries):
        return matmul(keys[pl.ds(pl.multiple_of(start, 128), count), :], block_queries)

    def absorb(carry, sc, parts):
        peak, total_ = carry
        top = jnp.max(sc, axis=0, keepdims=True)
        if peak is not None:
            top = jnp.maximum(peak, top)
        weights = jnp.exp2(sc - top).astype(BF16)
        if peak is not None:
            total_ = total_ * jnp.exp2(peak - top)
        at = 0
        for start, count in parts:
            add = matmul(vals[:88, pl.ds(pl.multiple_of(start, 128), count)], weights[at : at + count])
            total_ = add if total_ is None else total_ + add
            at += count
        return top, total_

    common = 4 * chip
    chunk1 = 512

    def first_phase(yk):
        todo = [(j, common + i * chunk1) for j in range(3) for i in range((WINDOW - common) // chunk1)]
        per = len(todo) // 3

        def make(t):
            j, start = todo[t]
            return scores(start, chunk1, queries[yk, :, j * 512 : (j + 1) * 512])

        sc = make(0)
        carry = (None, None)
        for t in range(len(todo)):
            later = make(t + 1) if t + 1 < len(todo) else None
            j, start = todo[t]
            carry = absorb(carry, sc, [(start, chunk1)])
            if t % per == per - 1:
                cols = slice(j * 512, (j + 1) * 512)
                maxes[yk, :, cols] = carry[0]
                state[yk, :, cols] = carry[1]
                carry = (None, None)
            sc = later

    def second_phase(yk):
        base = yk * chip
        full = [
            jnp.where(yk + i < 3, base + (i + 1) * chip, WINDOW + (i - (3 - yk)) * chip) for i in range(3)
        ]

        def make(j, u):
            block_queries = queries[yk, :, j * 512 : (j + 1) * 512]
            if u < 3:
                return scores(full[u], chip, block_queries)
            lowest, upto = chip - j * 128, (j + 1) * 128
            row = lax.broadcasted_iota(jnp.int32, (128, 512), 0)
            col = lax.broadcasted_iota(jnp.int32, (128, 512), 1) & (QBLOCK - 1)
            low = scores(base + j * 128, lowest, block_queries)
            high = scores(WINDOW + base, upto, block_queries)
            parts = [jnp.where(row > col, low[:128], HIDE), low[128:], high[:-128], jnp.where(row <= col, high[-128:], HIDE)]
            return jnp.concatenate([p for p in parts if p.shape[0]], axis=0)

        units = [(j, u) for j in range(3) for u in range(4)]
        sc = make(*units[0])
        for t, (j, u) in enumerate(units):
            later = make(*units[t + 1]) if t + 1 < len(units) else None
            cols = slice(j * 512, (j + 1) * 512)
            if u == 0:
                carry = (maxes[yk, :, cols], state[yk, :, cols])
            if u < 3:
                parts = [(full[u], chip)]
            else:
                parts = [(base + j * 128, chip - j * 128), (WINDOW + base, (j + 1) * 128)]
            carry = absorb(carry, sc, parts)
            if u == 3:
                sums = carry[1]
                attended = sums[:HEAD_DIM] * (1.0 / sums[HEAD_DIM : HEAD_DIM + 1])
                token = base + j * 128 + (lax.broadcasted_iota(jnp.int32, (HEAD_DIM, 512), 1) & (QBLOCK - 1))
                attended = jnp.where(token < length, attended, 0.0)
                heads = [attended[:, g * 128 : (g + 1) * 128] for g in range(GROUP)]
                if j == 1:
                    left = lax.broadcasted_iota(jnp.int32, (HEAD_DIM, 128), 1) < 64
                    for p in range(2):
                        one, two = heads[p], heads[p + 2]
                        at = slice(320 + p * HEAD_DIM, 320 + (p + 1) * HEAD_DIM)
                        ready[yk, 0, at, :] = jnp.where(left, one, pltpu.roll(two, 64, 1)).astype(BF16)
                        ready[yk, 1, at, :] = jnp.where(left, pltpu.roll(one, 64, 1), two).astype(BF16)
                else:
                    for g in range(GROUP):
                        ready[yk, j // 2, g * HEAD_DIM : (g + 1) * HEAD_DIM, :] = heads[g].astype(BF16)
            sc = later

    def arrive(k):
        @pl.when(k == 1)
        def _():
            y_copy(2, row_block(-1, c, half, half), 0, c).wait_recv()
            y_copy(8, row_block(-1, c, half, half), 0, 1 - c).start()
            y_copy(4, row_block(1, c, 0, half), 0, c).wait_recv()
            y_copy(10, row_block(1, c, 0, half), 0, 1 - c).start()
            gather_o.second_step()
            y_copy(7, row_block(-1, 1 - c, 0, half), 0, c).wait_recv()
            y_copy(8, row_block(-1, 1 - c, half, half), 0, c).wait_recv()

        @pl.when(k == 2)
        def _():
            gather_o.third_step()
            y_copy(9, row_block(1, 1 - c, half, half), 0, c).wait_recv()
            y_copy(10, row_block(1, 1 - c, 0, half), 0, c).wait_recv()

        @pl.when(k == 3)
        def _():
            y_copy(5, row_block(2, c, 0, half), 0, c).wait_recv()
            y_copy(6, row_block(2, c, half, half), 0, c).wait_recv()
            y_copy(11, row_block(2, c), 0, 1 - c).start()
            gather_o.fourth_step((0,))
            for q in range(1, 4):
                partner_copy(slot(turns[q], 0), c).start()
            y_copy(11, row_block(2, 1 - c), 0, c).wait_recv()

    def first_loop(k, carry):
        arrive(k)
        turn = jnp.where(k == 0, 0, jnp.where(k == 1, 3, k - 1))
        yk = lax.rem(y + turn, 4)
        project(yk)
        first_phase(yk)
        return carry

    lax.fori_loop(0, 4, first_loop, 0)

    def attended_copy(yk, core):
        return remote(
            ready.at[yk, core], received.at[h], a_send.at[2 * yk + core], a_recv.at[h], s, 2 * yk + core
        )

    def second_loop(k, carry):
        turn = jnp.where(k == 0, 2, jnp.where(k == 1, 1, jnp.where(k == 2, 3, 0)))
        yk = lax.rem(y + turn, 4)

        @pl.when(k == 0)
        def _():
            gather_o.fourth_step((1, 2))

        @pl.when(k == 1)
        def _():
            gather_o.fourth_step((3,))
            for q in range(4):
                partner_copy(slot(turns[q], -1), c).start()
                partner_copy(slot(turns[q], 1), c).start()

        @pl.when(k == 3)
        def _():
            gather_o.last_step()
            for q in range(4):
                partner_copy(slot(turns[q], 2), c).start()

        second_phase(yk)

        @pl.when(k < 3)
        def _():
            attended_copy(yk, 0).start()
            attended_copy(yk, 1).start()

        @pl.when(k == 3)
        def _():
            attended_copy(yk, 1 - c).start()

        return carry

    lax.fori_loop(0, 4, second_loop, 0)

    def unpack(src_head, block):
        top = src_head * GROUP * HEAD_DIM
        landed[pl.ds(pl.multiple_of(top, 16), GROUP * HEAD_DIM), :128] = block[: GROUP * HEAD_DIM]
        packed = block[GROUP * HEAD_DIM :]
        landed[pl.ds(pl.multiple_of(top, 16), 2 * HEAD_DIM), 128:] = packed
        turned_back = pltpu.roll(packed.astype(F32), 64, 1).astype(BF16)
        landed[pl.ds(pl.multiple_of(top + 2 * HEAD_DIM, 16), 2 * HEAD_DIM), 128:] = turned_back

    unpack(h, ready[y, c])
    for d in range(1, 16):
        sl = lax.rem(s + d, 16)
        partner_copy(sl, 1 - c).wait_recv()

    for dy, core in ((0, 1 - c), (2, 0), (2, 1), (1, 0), (1, 1), (-1, 0), (-1, 1)):
        src = head_of(dy, core)
        remote(received.at[src], received.at[src], a_send.at[0], a_recv.at[src], s, h).wait_recv()
        unpack(src, received[src])
    for i in range(width // 512):
        turned[:, i * 512 : (i + 1) * 512] = jnp.transpose(matmul(wo[i * 512 : (i + 1) * 512, :], landed[...]))
    rest = own - 128
    out[pl.ds(pl.multiple_of(c * rest, 64), 128), :] = turned[:128, :].astype(BF16)
    out[pl.ds(pl.multiple_of((1 - c) * 128, 64), rest), :] = turned[128:own, :].astype(BF16)

    for gather_q in gathers_q:
        gather_q.drain()
    gather_o.drain()
    for d in range(1, 16):
        partner_copy(lax.rem(s + d, 16), c).wait_send()
    for m in (0, 11):
        y_copy(m, row_block(0, c), 0, 1 - c).wait_send()
    for m in range(1, 11):
        y_copy(m, row_block(0, c, 0, half), 0, 1 - c).wait_send()
    for d in range(1, 8):
        dst = lax.rem(h + d, 8)
        remote(received.at[0], received.at[0], a_send.at[dst], a_recv.at[0], s, dst).wait_send()


def solution(mesh):
    def step(hidden, norm_gain, w_qkv, w_out, kv_cache, new_len, prefix_len):
        s, h = lax.axis_index("seq"), lax.axis_index("head")
        own, width = hidden.shape[1], hidden.shape[2]
        new_total = 8 * own
        wide = (GROUP + 2) * HEAD_DIM
        piece = w_qkv.shape[0]
        w_mine = lax.dynamic_slice(w_qkv, (0, h * wide), (piece, wide))
        wo_mine = w_out.T
        cached = jnp.swapaxes(kv_cache.reshape(WINDOW, 2 * HEAD_DIM), 0, 1)
        frequency = np.exp(np.arange(HALF, dtype=np.float64) * (-2.0 * math.log(10000.0) / HEAD_DIM))
        angles = frequency[:, None] * np.arange(new_total, dtype=np.float64)[None, :]
        cos_slot = jnp.asarray(np.cos(angles).astype(np.float32))
        sin_slot = jnp.asarray(np.sin(angles).astype(np.float32))
        lanes = jnp.asarray(np.broadcast_to(frequency[:, None], (HALF, 128)).astype(np.float32))
        chip = 2 * own
        dma = pltpu.SemaphoreType.DMA
        vmem = pl.BlockSpec(memory_space=pltpu.VMEM)
        smem = pl.BlockSpec(memory_space=pltpu.SMEM)
        any_ = pl.BlockSpec(memory_space=pl.ANY)
        attn_out, kv_written = pl.pallas_call(
            kernel,
            out_shape=(
                pltpu.VMEM((own, width), BF16),
                pltpu.VMEM((2 * HEAD_DIM, new_total), BF16),
            ),
            in_specs=[any_, vmem, any_, any_, any_, any_, any_, vmem, smem, smem],
            out_specs=(vmem, vmem),
            scratch_shapes=[
                pltpu.VMEM((own, width), BF16),
                pltpu.VMEM((HALF, new_total), F32),
                pltpu.VMEM((HALF, new_total), F32),
                pltpu.VMEM((HEAD_DIM, WINDOW), BF16),
                pltpu.VMEM((4, chip, width), BF16),
                pltpu.VMEM((16 * piece, wide), BF16),
                pltpu.VMEM((16 * piece, width), BF16),
                pltpu.VMEM((WINDOW + new_total, 256), BF16),
                pltpu.VMEM((96, WINDOW + new_total), BF16),
                pltpu.VMEM((4, 256, 4 * chip), BF16),
                pltpu.VMEM((4, 88, 4 * chip), F32),
                pltpu.VMEM((4, 1, 4 * chip), F32),
                pltpu.VMEM((4, 2, 6 * HEAD_DIM, 128), BF16),
                pltpu.VMEM((8, 6 * HEAD_DIM, 128), BF16),
                pltpu.VMEM((8 * GROUP * HEAD_DIM, 256), BF16),
                pltpu.VMEM((256, width), F32),
                dma((7,)), dma((20 * len(SPLITS),)), dma((20 * len(SPLITS),)), dma((20,)), dma((20,)), dma((16,)), dma((16,)),
                dma((12,)), dma((12,)), dma((8,)), dma((8,)),
            ],
            compiler_params=pltpu.CompilerParams(
                collective_id=0, has_side_effects=True, vmem_limit_bytes=56 * 1024 * 1024
            ),
        )(
            hidden.reshape(own, width), norm_gain, w_mine, wo_mine,
            cached, cos_slot, sin_slot, lanes, new_len, prefix_len,
        )
        return attn_out.reshape(1, own, width), jnp.swapaxes(kv_written, 0, 1).reshape(1, new_total, 2 * HEAD_DIM)

    return jax.shard_map(
        step,
        mesh=mesh,
        in_specs=(
            P("seq", "head", None), P(), P("seq", None), P(None, "seq"), P("seq", None, "head"), P(), P(),
        ),
        out_specs=(P("seq", "head", None), P("seq", None, "head")),
        check_vma=False,
    )
```

```python
import math

import jax
import jax.numpy as jnp
import numpy as np
from jax import lax
from jax.experimental import pallas as pl
from jax.experimental.pallas import tpu as pltpu
from jax.sharding import PartitionSpec as P

HEAD_DIM = 80
HALF = HEAD_DIM // 2
GROUP = 4
WINDOW = 4096
QBLOCK = 128
COLS1, KEYS1 = 768, 512
SPLITS = ((80, 80),)
HIDE = -(2.0**127)
F32 = jnp.float32
BF16 = jnp.bfloat16
MESH = pl.DeviceIdType.MESH


def matmul(a, b):
    return lax.dot_general(a, b, (((1,), (0,)), ((), ())), preferred_element_type=F32)


def kernel(
    hidden_hbm, gain, w_mine, wo_mine, kv_hbm, cos_hbm, sin_hbm, frequency, new_len, prefix_len,
    out, written,
    hidden, cos_slot, sin_slot, cached_keys,
    rows, wq, wo, keys, vals, queries, state, maxes, ready, received, landed, turned,
    local, w_send, w_recv, o_send, o_recv, p_send, p_recv, y_send, y_recv, a_send, a_recv,
):
    s = lax.axis_index("seq")
    h = lax.axis_index("head")
    y, c = h // 2, h % 2
    own = hidden.shape[0]
    chip = 2 * own
    width = hidden.shape[1]
    piece = w_mine.shape[0]
    half_o = piece // 2
    length, prefix = new_len[s], prefix_len[s]
    x, z = s // 4, s % 4
    a, b = x + c * (z - x), z + c * (x - z)
    step_a, step_b = 4 - 3 * c, 1 + 3 * c

    fetches = []

    def fetch(src, dst):
        copy = pltpu.make_async_copy(src, dst, local.at[len(fetches)])
        copy.start()
        fetches.append(copy)
        return copy

    got_hidden = fetch(hidden_hbm, hidden)
    got_wq = fetch(w_mine, wq.at[pl.ds(pl.multiple_of(s * piece, 16), piece)])
    got_keys = fetch(kv_hbm.at[pl.ds(0, HEAD_DIM)], cached_keys)
    got_vals = fetch(kv_hbm.at[pl.ds(HEAD_DIM, HEAD_DIM)], vals.at[pl.ds(0, HEAD_DIM), pl.ds(0, WINDOW)])
    got_wo = fetch(wo_mine, wo.at[pl.ds(pl.multiple_of(s * piece, 16), piece)])
    got_cos = fetch(cos_hbm, cos_slot)
    got_sin = fetch(sin_hbm, sin_slot)

    def slot(da, db):
        return lax.rem(a + da + 4, 4) * step_a + lax.rem(b + db + 4, 4) * step_b

    def head_of(dy, core):
        return lax.rem(y + dy + 4, 4) * 2 + core

    def remote(src, dst, send, recv, seq_id, head_id):
        return pltpu.make_async_remote_copy(
            src_ref=src, dst_ref=dst, send_sem=send, recv_sem=recv,
            device_id={"seq": seq_id, "head": head_id}, device_id_type=MESH,
        )

    barrier = pltpu.get_barrier_semaphore()
    for da, db in ((1, 0), (-1, 0), (2, 0), (0, 1), (0, -1)):
        pl.semaphore_signal(barrier, inc=1, device_id={"seq": slot(da, db), "head": h}, device_id_type=MESH)
    for d in range(1, 8):
        pl.semaphore_signal(barrier, inc=1, device_id={"seq": s, "head": lax.rem(h + d, 8)}, device_id_type=MESH)
    pl.semaphore_wait(barrier, 12)

    turns = (0, -1, 1, 2)

    class Gather:
        def __init__(self, mine, whole, first, second, send, recv, at=0, direct=False):
            self.mine, self.whole, self.first, self.second = mine, whole, first, second
            self.send, self.recv, self.at, self.direct = send, recv, at, direct

        def copy(self, m, src, dst, da, db):
            return remote(src, dst, self.send.at[self.at + m], self.recv.at[self.at + m], slot(da, db), h)

        def start_a(self):
            me = self.whole(slot(0, 0))
            self.copy(0, self.mine, me, 1, 0).start()
            self.copy(1, self.mine, me, -1, 0).start()
            if self.direct:
                self.copy(2, self.mine, me, 2, 0).start()

        def start_b(self):
            me = self.whole(slot(0, 0))
            self.copy(4, self.mine, me, 0, 1).start()
            self.copy(5, self.mine, me, 0, -1).start()

        def got(self, m, region):
            self.copy(m, region, region, 1, 0).wait_recv()

        def forward_b(self, q):
            region = self.whole(slot(turns[q], 0))
            self.copy(4 + 2 * q, region, region, 0, 1).start()
            self.copy(5 + 2 * q, region, region, 0, -1).start()

        def second_step(self):
            self.got(0, self.whole(slot(-1, 0)))
            self.got(1, self.whole(slot(1, 0)))
            if not self.direct:
                ra, rb = self.first(slot(-1, 0)), self.second(slot(1, 0))
                self.copy(2, ra, ra, 1, 0).start()
                self.copy(3, rb, rb, -1, 0).start()
            self.forward_b(1)
            self.forward_b(2)

        def third_step(self):
            if self.direct:
                self.got(2, self.whole(slot(2, 0)))
            else:
                self.got(2, self.first(slot(2, 0)))
                self.got(3, self.second(slot(2, 0)))
            self.forward_b(3)

        def fourth_step(self, shards):
            for q in shards:
                self.got(4 + 2 * q, self.whole(slot(turns[q], -1)))
                self.got(5 + 2 * q, self.whole(slot(turns[q], 1)))
                ra, rb = self.first(slot(turns[q], -1)), self.second(slot(turns[q], 1))
                self.copy(12 + 2 * q, ra, ra, 0, 1).start()
                self.copy(13 + 2 * q, rb, rb, 0, -1).start()

        def last_step(self):
            for q in range(4):
                self.got(12 + 2 * q, self.first(slot(turns[q], 2)))
                self.got(13 + 2 * q, self.second(slot(turns[q], 2)))

        def drain(self):
            me = self.mine
            for m in (0, 1, 2, 4, 5) if self.direct else (0, 1, 4, 5):
                self.copy(m, me, me, 1, 0).wait_send()
            for m in (12, 14, 16, 18) if self.direct else (2, 12, 14, 16, 18):
                r = self.first(slot(0, 0))
                self.copy(m, r, r, 1, 0).wait_send()
            for m in (13, 15, 17, 19) if self.direct else (3, 13, 15, 17, 19):
                r = self.second(slot(0, 0))
                self.copy(m, r, r, 1, 0).wait_send()
            for m in (6, 7, 8, 9, 10, 11):
                r = self.whole(slot(0, 0))
                self.copy(m, r, r, 1, 0).wait_send()

    def wq_rows(offset, count):
        return lambda sl: wq.at[pl.ds(pl.multiple_of(sl * piece + offset, 16), count)]

    gathers_q, at = [], 0
    for i, (one, two) in enumerate(SPLITS):
        gathers_q.append(
            Gather(
                wq_rows(at, one + two)(s), wq_rows(at, one + two), wq_rows(at, one), wq_rows(at + one, two),
                w_send, w_recv, 20 * i, direct=True,
            )
        )
        at += one + two

    def wo_part(core, lo, count):
        return lambda sl: wo.at[
            pl.ds(pl.multiple_of(sl * piece + core * half_o, 16), half_o), pl.ds(lo, count)
        ]

    gather_o = Gather(
        wo_mine.at[pl.ds(pl.multiple_of(c * half_o, 16), half_o)],
        wo_part(c, 0, width), wo_part(c, 0, width // 2), wo_part(c, width // 2, width // 2), o_send, o_recv,
    )

    def partner_copy(sl, core):
        region = wo_part(core, 0, width)(sl)
        return remote(region, region, p_send.at[sl], p_recv.at[sl], s, head_of(0, 1 - c))

    got_wq.wait()
    for gather_q in gathers_q:
        gather_q.start_a()
        gather_q.start_b()
    got_hidden.wait()

    def row_block(dy, core, offset=0, count=own):
        return rows.at[lax.rem(y + dy + 4, 4), pl.ds(pl.multiple_of(core * own + offset, 16), count)]

    def norm_rows(i, carry):
        values = hidden[pl.ds(pl.multiple_of(i * 32, 32), 32), :].astype(F32)
        meansq = jnp.mean(values * values, axis=-1, keepdims=True)
        normed = (values * lax.rsqrt(meansq + 1e-05) * gain[...].reshape(1, width)).astype(BF16)
        rows[y, pl.ds(pl.multiple_of(c * own + i * 32, 32), 32), :] = normed
        return carry


    def y_copy(m, region, dy, core):
        return remote(region, region, y_send.at[m], y_recv.at[m], s, head_of(dy, core))

    half = own // 2
    lax.fori_loop(0, half // 32, norm_rows, 0)
    y_copy(1, row_block(0, c, 0, half), 1, c).start()
    lax.fori_loop(half // 32, own // 32, norm_rows, 0)
    y_copy(3, row_block(0, c, half, half), -1, c).start()
    y_copy(2, row_block(0, c, half, half), 1, c).start()
    y_copy(4, row_block(0, c, 0, half), -1, c).start()
    y_copy(0, row_block(0, c), 0, 1 - c).start()

    for gather_q in gathers_q:
        gather_q.second_step()
    got_keys.wait()

    def prepare_cache(i, carry):
        at = pl.ds(pl.multiple_of(i * 256, 256), 256)
        token = i * 256 + lax.broadcasted_iota(jnp.int32, (48, 256), 1)
        first = lax.broadcasted_iota(jnp.int32, (48, 256), 0) == 0
        bias = jnp.where(first & (token < WINDOW - prefix), HIDE, 0.0)
        block = jnp.transpose(jnp.concatenate([cached_keys[:, at].astype(F32), bias], axis=0))
        lane = lax.broadcasted_iota(jnp.int32, (256, 128), 1)
        keys[at, :128] = block.astype(BF16)
        keys[at, 128:] = jnp.where(lane < HEAD_DIM, block, 0.0).astype(BF16)
        return carry

    lax.fori_loop(0, WINDOW // 256, prepare_cache, 0)
    for gather_q in gathers_q:
        gather_q.third_step()
    got_wo.wait()
    got_vals.wait()
    got_cos.wait()
    got_sin.wait()
    total = vals.shape[1]
    one_row = (lax.broadcasted_iota(jnp.int32, (16, 512), 0) == 0).astype(F32).astype(BF16)
    for i in range(total // 512):
        vals[HEAD_DIM:, i * 512 : (i + 1) * 512] = one_row
    for k in range(4):
        for i in range(3):
            cols = slice(i * 512, (i + 1) * 512)
            queries[k, 80:96, cols] = one_row
            queries[k, 96:128, cols] = jnp.zeros((32, 512), BF16)
            queries[k, 208:256, cols] = jnp.zeros((48, 512), BF16)
    turn_pre = frequency[...] * prefix.astype(F32)
    cp, sp = jnp.cos(turn_pre)[:, 0:1], jnp.sin(turn_pre)[:, 0:1]

    for gather_q in gathers_q:
        gather_q.fourth_step(range(4))
    gather_o.start_a()
    y_copy(0, row_block(0, 1 - c), 0, c).wait_recv()
    y_copy(1, row_block(-1, c, 0, half), 0, c).wait_recv()
    y_copy(5, row_block(-1, c, 0, half), 1, c).start()
    y_copy(3, row_block(1, c, half, half), 0, c).wait_recv()
    y_copy(6, row_block(1, c, half, half), -1, c).start()
    y_copy(7, row_block(-1, c, 0, half), 0, 1 - c).start()
    y_copy(9, row_block(1, c, half, half), 0, 1 - c).start()
    for gather_q in gathers_q:
        gather_q.last_step()
    gather_o.start_b()

    scale = math.log2(math.e) / math.sqrt(HEAD_DIM)

    def project(yk):
        projected = jnp.transpose(matmul(rows[yk], wq[...]))
        tokens = pl.ds(pl.multiple_of(yk * chip, 128), chip)
        cn, sn = cos_slot[:, tokens], sin_slot[:, tokens]
        cosine, sine = cn * cp - sn * sp, sn * cp + cn * sp

        def rotate(at):
            lead, trail = projected[at : at + HALF], projected[at + HALF : at + HEAD_DIM]
            turned = jnp.concatenate([lead * cosine - trail * sine, trail * cosine + lead * sine], axis=0)
            return turned.astype(BF16).astype(F32)

        for g in range(GROUP):
            scaled = rotate(g * HEAD_DIM) * scale
            high = scaled.astype(BF16)
            low = (scaled - high.astype(F32)).astype(BF16)
            for j in range(3):
                cols = slice(j * 512 + g * 128, j * 512 + g * 128 + 128)
                toks = slice(j * 128, j * 128 + 128)
                queries[yk, 0:80, cols] = high[:, toks]
                queries[yk, 128:208, cols] = low[:, toks]
        key = rotate(GROUP * HEAD_DIM)
        value = projected[(GROUP + 1) * HEAD_DIM : (GROUP + 2) * HEAD_DIM].astype(BF16)
        slots = pl.ds(pl.multiple_of(WINDOW + yk * chip, 128), chip)
        vals[:HEAD_DIM, slots] = value
        pair = jnp.concatenate([key, value.astype(F32)], axis=0)
        index = yk * chip + lax.broadcasted_iota(jnp.int32, pair.shape, 1)
        written[:, tokens] = jnp.where(index < length, pair, 0.0).astype(BF16)
        clean = jnp.transpose(jnp.concatenate([key, jnp.zeros((48, chip), F32)], axis=0)).astype(BF16)
        keys[slots, :128] = clean
        keys[slots, 128:] = clean

    def scores(start, count, block_queries):
        return matmul(keys[pl.ds(pl.multiple_of(start, 128), count), :], block_queries)

    def absorb(carry, sc, parts):
        peak, total_ = carry
        top = jnp.max(sc, axis=0, keepdims=True)
        if peak is not None:
            top = jnp.maximum(peak, top)
        weights = jnp.exp2(sc - top).astype(BF16)
        if peak is not None:
            total_ = total_ * jnp.exp2(peak - top)
        at = 0
        for start, count in parts:
            add = matmul(vals[:88, pl.ds(pl.multiple_of(start, 128), count)], weights[at : at + count])
            total_ = add if total_ is None else total_ + add
            at += count
        return top, total_

    common = 4 * chip

    def first_phase(yk):
        keys_at = range(common, WINDOW, KEYS1)
        todo = [(at, start) for at in range(0, 4 * chip, COLS1) for start in keys_at]

        def make(t):
            at, start = todo[t]
            return scores(start, KEYS1, queries[yk, :, at : at + COLS1])

        sc = make(0)
        carry = (None, None)
        for t, (at, start) in enumerate(todo):
            later = make(t + 1) if t + 1 < len(todo) else None
            carry = absorb(carry, sc, [(start, KEYS1)])
            if start + KEYS1 == WINDOW:
                maxes[yk, :, at : at + COLS1] = carry[0]
                state[yk, :, at : at + COLS1] = carry[1]
                carry = (None, None)
            sc = later

    def second_phase(yk):
        base = yk * chip
        full = [
            jnp.where(yk + i < 3, base + (i + 1) * chip, WINDOW + (i - (3 - yk)) * chip) for i in range(3)
        ]

        def make(j, u):
            block_queries = queries[yk, :, j * 512 : (j + 1) * 512]
            if u < 3:
                return scores(full[u], chip, block_queries)
            lowest, upto = chip - j * 128, (j + 1) * 128
            row = lax.broadcasted_iota(jnp.int32, (128, 512), 0)
            col = lax.broadcasted_iota(jnp.int32, (128, 512), 1) & (QBLOCK - 1)
            low = scores(base + j * 128, lowest, block_queries)
            high = scores(WINDOW + base, upto, block_queries)
            parts = [jnp.where(row > col, low[:128], HIDE), low[128:], high[:-128], jnp.where(row <= col, high[-128:], HIDE)]
            return jnp.concatenate([p for p in parts if p.shape[0]], axis=0)

        units = [(j, u) for j in range(3) for u in range(4)]
        sc = make(*units[0])
        for t, (j, u) in enumerate(units):
            later = make(*units[t + 1]) if t + 1 < len(units) else None
            cols = slice(j * 512, (j + 1) * 512)
            if u == 0:
                carry = (maxes[yk, :, cols], state[yk, :, cols])
            if u < 3:
                parts = [(full[u], chip)]
            else:
                parts = [(base + j * 128, chip - j * 128), (WINDOW + base, (j + 1) * 128)]
            carry = absorb(carry, sc, parts)
            if u == 3:
                sums = carry[1]
                attended = sums[:HEAD_DIM] * (1.0 / sums[HEAD_DIM : HEAD_DIM + 1])
                token = base + j * 128 + (lax.broadcasted_iota(jnp.int32, (HEAD_DIM, 512), 1) & (QBLOCK - 1))
                attended = jnp.where(token < length, attended, 0.0)
                heads = [attended[:, g * 128 : (g + 1) * 128] for g in range(GROUP)]
                if j == 1:
                    left = lax.broadcasted_iota(jnp.int32, (HEAD_DIM, 128), 1) < 64
                    for p in range(2):
                        one, two = heads[p], heads[p + 2]
                        at = slice(320 + p * HEAD_DIM, 320 + (p + 1) * HEAD_DIM)
                        ready[yk, 0, at, :] = jnp.where(left, one, pltpu.roll(two, 64, 1)).astype(BF16)
                        ready[yk, 1, at, :] = jnp.where(left, pltpu.roll(one, 64, 1), two).astype(BF16)
                else:
                    for g in range(GROUP):
                        ready[yk, j // 2, g * HEAD_DIM : (g + 1) * HEAD_DIM, :] = heads[g].astype(BF16)
            sc = later

    def arrive(k):
        @pl.when(k == 1)
        def _():
            y_copy(2, row_block(-1, c, half, half), 0, c).wait_recv()
            y_copy(8, row_block(-1, c, half, half), 0, 1 - c).start()
            y_copy(4, row_block(1, c, 0, half), 0, c).wait_recv()
            y_copy(10, row_block(1, c, 0, half), 0, 1 - c).start()
            gather_o.second_step()
            y_copy(7, row_block(-1, 1 - c, 0, half), 0, c).wait_recv()
            y_copy(8, row_block(-1, 1 - c, half, half), 0, c).wait_recv()

        @pl.when(k == 2)
        def _():
            gather_o.third_step()
            y_copy(9, row_block(1, 1 - c, half, half), 0, c).wait_recv()
            y_copy(10, row_block(1, 1 - c, 0, half), 0, c).wait_recv()

        @pl.when(k == 3)
        def _():
            y_copy(5, row_block(2, c, 0, half), 0, c).wait_recv()
            y_copy(6, row_block(2, c, half, half), 0, c).wait_recv()
            y_copy(11, row_block(2, c), 0, 1 - c).start()
            gather_o.fourth_step((0,))
            for q in range(1, 4):
                partner_copy(slot(turns[q], 0), c).start()
            y_copy(11, row_block(2, 1 - c), 0, c).wait_recv()

    def first_loop(k, carry):
        arrive(k)
        turn = jnp.where(k == 0, 0, jnp.where(k == 1, 3, k - 1))
        yk = lax.rem(y + turn, 4)
        project(yk)
        first_phase(yk)
        return carry

    lax.fori_loop(0, 4, first_loop, 0)

    def attended_copy(yk, core):
        return remote(
            ready.at[yk, core], received.at[h], a_send.at[2 * yk + core], a_recv.at[h], s, 2 * yk + core
        )

    def second_loop(k, carry):
        turn = jnp.where(k == 0, 2, jnp.where(k == 1, 1, jnp.where(k == 2, 3, 0)))
        yk = lax.rem(y + turn, 4)

        @pl.when(k == 0)
        def _():
            gather_o.fourth_step((1, 2))

        @pl.when(k == 1)
        def _():
            gather_o.fourth_step((3,))
            for q in range(4):
                partner_copy(slot(turns[q], -1), c).start()
                partner_copy(slot(turns[q], 1), c).start()

        @pl.when(k == 3)
        def _():
            gather_o.last_step()
            for q in range(4):
                partner_copy(slot(turns[q], 2), c).start()

        second_phase(yk)

        @pl.when(k < 3)
        def _():
            attended_copy(yk, 0).start()
            attended_copy(yk, 1).start()

        @pl.when(k == 3)
        def _():
            attended_copy(yk, 1 - c).start()

        return carry

    lax.fori_loop(0, 4, second_loop, 0)

    def unpack(src_head, block):
        top = src_head * GROUP * HEAD_DIM
        landed[pl.ds(pl.multiple_of(top, 16), GROUP * HEAD_DIM), :128] = block[: GROUP * HEAD_DIM]
        packed = block[GROUP * HEAD_DIM :]
        landed[pl.ds(pl.multiple_of(top, 16), 2 * HEAD_DIM), 128:] = packed
        turned_back = pltpu.roll(packed.astype(F32), 64, 1).astype(BF16)
        landed[pl.ds(pl.multiple_of(top + 2 * HEAD_DIM, 16), 2 * HEAD_DIM), 128:] = turned_back

    unpack(h, ready[y, c])
    for d in range(1, 16):
        sl = lax.rem(s + d, 16)
        partner_copy(sl, 1 - c).wait_recv()

    for dy, core in ((0, 1 - c), (2, 0), (2, 1), (1, 0), (1, 1), (-1, 0), (-1, 1)):
        src = head_of(dy, core)
        remote(received.at[src], received.at[src], a_send.at[0], a_recv.at[src], s, h).wait_recv()
        unpack(src, received[src])
    for i in range(width // 512):
        turned[:, i * 512 : (i + 1) * 512] = jnp.transpose(matmul(wo[i * 512 : (i + 1) * 512, :], landed[...]))
    rest = own - 128
    out[pl.ds(pl.multiple_of(c * rest, 64), 128), :] = turned[:128, :].astype(BF16)
    out[pl.ds(pl.multiple_of((1 - c) * 128, 64), rest), :] = turned[128:own, :].astype(BF16)

    for gather_q in gathers_q:
        gather_q.drain()
    gather_o.drain()
    for d in range(1, 16):
        partner_copy(lax.rem(s + d, 16), c).wait_send()
    for m in (0, 11):
        y_copy(m, row_block(0, c), 0, 1 - c).wait_send()
    for m in range(1, 11):
        y_copy(m, row_block(0, c, 0, half), 0, 1 - c).wait_send()
    for d in range(1, 8):
        dst = lax.rem(h + d, 8)
        remote(received.at[0], received.at[0], a_send.at[dst], a_recv.at[0], s, dst).wait_send()


def solution(mesh):
    def step(hidden, norm_gain, w_qkv, w_out, kv_cache, new_len, prefix_len):
        s, h = lax.axis_index("seq"), lax.axis_index("head")
        own, width = hidden.shape[1], hidden.shape[2]
        new_total = 8 * own
        wide = (GROUP + 2) * HEAD_DIM
        piece = w_qkv.shape[0]
        w_mine = lax.dynamic_slice(w_qkv, (0, h * wide), (piece, wide))
        wo_mine = w_out.T
        cached = jnp.swapaxes(kv_cache.reshape(WINDOW, 2 * HEAD_DIM), 0, 1)
        frequency = np.exp(np.arange(HALF, dtype=np.float64) * (-2.0 * math.log(10000.0) / HEAD_DIM))
        angles = frequency[:, None] * np.arange(new_total, dtype=np.float64)[None, :]
        cos_slot = jnp.asarray(np.cos(angles).astype(np.float32))
        sin_slot = jnp.asarray(np.sin(angles).astype(np.float32))
        lanes = jnp.asarray(np.broadcast_to(frequency[:, None], (HALF, 128)).astype(np.float32))
        chip = 2 * own
        dma = pltpu.SemaphoreType.DMA
        vmem = pl.BlockSpec(memory_space=pltpu.VMEM)
        smem = pl.BlockSpec(memory_space=pltpu.SMEM)
        any_ = pl.BlockSpec(memory_space=pl.ANY)
        attn_out, kv_written = pl.pallas_call(
            kernel,
            out_shape=(
                pltpu.VMEM((own, width), BF16),
                pltpu.VMEM((2 * HEAD_DIM, new_total), BF16),
            ),
            in_specs=[any_, vmem, any_, any_, any_, any_, any_, vmem, smem, smem],
            out_specs=(vmem, vmem),
            scratch_shapes=[
                pltpu.VMEM((own, width), BF16),
                pltpu.VMEM((HALF, new_total), F32),
                pltpu.VMEM((HALF, new_total), F32),
                pltpu.VMEM((HEAD_DIM, WINDOW), BF16),
                pltpu.VMEM((4, chip, width), BF16),
                pltpu.VMEM((16 * piece, wide), BF16),
                pltpu.VMEM((16 * piece, width), BF16),
                pltpu.VMEM((WINDOW + new_total, 256), BF16),
                pltpu.VMEM((96, WINDOW + new_total), BF16),
                pltpu.VMEM((4, 256, 4 * chip), BF16),
                pltpu.VMEM((4, 88, 4 * chip), F32),
                pltpu.VMEM((4, 1, 4 * chip), F32),
                pltpu.VMEM((4, 2, 6 * HEAD_DIM, 128), BF16),
                pltpu.VMEM((8, 6 * HEAD_DIM, 128), BF16),
                pltpu.VMEM((8 * GROUP * HEAD_DIM, 256), BF16),
                pltpu.VMEM((256, width), F32),
                dma((7,)), dma((20 * len(SPLITS),)), dma((20 * len(SPLITS),)), dma((20,)), dma((20,)), dma((16,)), dma((16,)),
                dma((12,)), dma((12,)), dma((8,)), dma((8,)),
            ],
            compiler_params=pltpu.CompilerParams(
                collective_id=0, has_side_effects=True, vmem_limit_bytes=56 * 1024 * 1024
            ),
        )(
            hidden.reshape(own, width), norm_gain, w_mine, wo_mine,
            cached, cos_slot, sin_slot, lanes, new_len, prefix_len,
        )
        return attn_out.reshape(1, own, width), jnp.swapaxes(kv_written, 0, 1).reshape(1, new_total, 2 * HEAD_DIM)

    return jax.shard_map(
        step,
        mesh=mesh,
        in_specs=(
            P("seq", "head", None), P(), P("seq", None), P(None, "seq"), P("seq", None, "head"), P(), P(),
        ),
        out_specs=(P("seq", "head", None), P("seq", None, "head")),
        check_vma=False,
    )
```

```python
import math

import jax
import jax.numpy as jnp
import numpy as np
from jax import lax
from jax.experimental import pallas as pl
from jax.experimental.pallas import tpu as pltpu
from jax.sharding import PartitionSpec as P

HEAD_DIM = 80
HALF = HEAD_DIM // 2
GROUP = 4
WINDOW = 4096
QBLOCK = 128
COLS1, KEYS1 = 768, 512
SPLITS = ((80, 80),)
HIDE = -(2.0**127)
F32 = jnp.float32
BF16 = jnp.bfloat16
MESH = pl.DeviceIdType.MESH


def matmul(a, b):
    return lax.dot_general(a, b, (((1,), (0,)), ((), ())), preferred_element_type=F32)


def kernel(
    hidden_hbm, gain, w_mine, wo_mine, kv_hbm, cos_hbm, sin_hbm, frequency, new_len, prefix_len,
    out, written,
    hidden, cos_slot, sin_slot, cached_keys,
    rows, wq, wo, keys, vals, queries, state, maxes, ready, received, landed, turned,
    local, w_send, w_recv, o_send, o_recv, p_send, p_recv, y_send, y_recv, a_send, a_recv,
):
    s = lax.axis_index("seq")
    h = lax.axis_index("head")
    y, c = h // 2, h % 2
    own = hidden.shape[0]
    chip = 2 * own
    width = hidden.shape[1]
    piece = w_mine.shape[0]
    half_o = piece // 2
    length, prefix = new_len[s], prefix_len[s]
    x, z = s // 4, s % 4
    a, b = x + c * (z - x), z + c * (x - z)
    step_a, step_b = 4 - 3 * c, 1 + 3 * c

    fetches = []

    def fetch(src, dst):
        copy = pltpu.make_async_copy(src, dst, local.at[len(fetches)])
        copy.start()
        fetches.append(copy)
        return copy

    got_hidden = fetch(hidden_hbm, hidden)
    got_wq = fetch(w_mine, wq.at[pl.ds(pl.multiple_of(s * piece, 16), piece)])
    got_keys = fetch(kv_hbm.at[pl.ds(0, HEAD_DIM)], cached_keys)
    got_vals = fetch(kv_hbm.at[pl.ds(HEAD_DIM, HEAD_DIM)], vals.at[pl.ds(0, HEAD_DIM), pl.ds(0, WINDOW)])
    got_wo = fetch(wo_mine, wo.at[pl.ds(pl.multiple_of(s * piece, 16), piece)])
    got_cos = fetch(cos_hbm, cos_slot)
    got_sin = fetch(sin_hbm, sin_slot)

    def slot(da, db):
        return lax.rem(a + da + 4, 4) * step_a + lax.rem(b + db + 4, 4) * step_b

    def head_of(dy, core):
        return lax.rem(y + dy + 4, 4) * 2 + core

    def remote(src, dst, send, recv, seq_id, head_id):
        return pltpu.make_async_remote_copy(
            src_ref=src, dst_ref=dst, send_sem=send, recv_sem=recv,
            device_id={"seq": seq_id, "head": head_id}, device_id_type=MESH,
        )

    barrier = pltpu.get_barrier_semaphore()
    for da, db in ((1, 0), (-1, 0), (2, 0), (0, 1), (0, -1)):
        pl.semaphore_signal(barrier, inc=1, device_id={"seq": slot(da, db), "head": h}, device_id_type=MESH)
    for d in range(1, 8):
        pl.semaphore_signal(barrier, inc=1, device_id={"seq": s, "head": lax.rem(h + d, 8)}, device_id_type=MESH)
    pl.semaphore_wait(barrier, 12)

    turns = (0, -1, 1, 2)

    class Gather:
        def __init__(self, mine, whole, first, second, send, recv, at=0, direct=False):
            self.mine, self.whole, self.first, self.second = mine, whole, first, second
            self.send, self.recv, self.at, self.direct = send, recv, at, direct

        def copy(self, m, src, dst, da, db):
            return remote(src, dst, self.send.at[self.at + m], self.recv.at[self.at + m], slot(da, db), h)

        def start_a(self):
            me = self.whole(slot(0, 0))
            self.copy(0, self.mine, me, 1, 0).start()
            self.copy(1, self.mine, me, -1, 0).start()
            if self.direct:
                self.copy(2, self.mine, me, 2, 0).start()

        def start_b(self):
            me = self.whole(slot(0, 0))
            self.copy(4, self.mine, me, 0, 1).start()
            self.copy(5, self.mine, me, 0, -1).start()

        def got(self, m, region):
            self.copy(m, region, region, 1, 0).wait_recv()

        def forward_b(self, q):
            region = self.whole(slot(turns[q], 0))
            self.copy(4 + 2 * q, region, region, 0, 1).start()
            self.copy(5 + 2 * q, region, region, 0, -1).start()

        def second_step(self):
            self.got(0, self.whole(slot(-1, 0)))
            self.got(1, self.whole(slot(1, 0)))
            if not self.direct:
                ra, rb = self.first(slot(-1, 0)), self.second(slot(1, 0))
                self.copy(2, ra, ra, 1, 0).start()
                self.copy(3, rb, rb, -1, 0).start()
            self.forward_b(1)
            self.forward_b(2)

        def third_step(self):
            if self.direct:
                self.got(2, self.whole(slot(2, 0)))
            else:
                self.got(2, self.first(slot(2, 0)))
                self.got(3, self.second(slot(2, 0)))
            self.forward_b(3)

        def fourth_step(self, shards):
            for q in shards:
                self.got(4 + 2 * q, self.whole(slot(turns[q], -1)))
                self.got(5 + 2 * q, self.whole(slot(turns[q], 1)))
                ra, rb = self.first(slot(turns[q], -1)), self.second(slot(turns[q], 1))
                self.copy(12 + 2 * q, ra, ra, 0, 1).start()
                self.copy(13 + 2 * q, rb, rb, 0, -1).start()

        def last_step(self):
            for q in range(4):
                self.got(12 + 2 * q, self.first(slot(turns[q], 2)))
                self.got(13 + 2 * q, self.second(slot(turns[q], 2)))

        def drain(self):
            me = self.mine
            for m in (0, 1, 2, 4, 5) if self.direct else (0, 1, 4, 5):
                self.copy(m, me, me, 1, 0).wait_send()
            for m in (12, 14, 16, 18) if self.direct else (2, 12, 14, 16, 18):
                r = self.first(slot(0, 0))
                self.copy(m, r, r, 1, 0).wait_send()
            for m in (13, 15, 17, 19) if self.direct else (3, 13, 15, 17, 19):
                r = self.second(slot(0, 0))
                self.copy(m, r, r, 1, 0).wait_send()
            for m in (6, 7, 8, 9, 10, 11):
                r = self.whole(slot(0, 0))
                self.copy(m, r, r, 1, 0).wait_send()

    def wq_rows(offset, count):
        return lambda sl: wq.at[pl.ds(pl.multiple_of(sl * piece + offset, 16), count)]

    gathers_q, at = [], 0
    for i, (one, two) in enumerate(SPLITS):
        gathers_q.append(
            Gather(
                wq_rows(at, one + two)(s), wq_rows(at, one + two), wq_rows(at, one), wq_rows(at + one, two),
                w_send, w_recv, 20 * i, direct=True,
            )
        )
        at += one + two

    def wo_part(core, lo, count):
        return lambda sl: wo.at[
            pl.ds(pl.multiple_of(sl * piece + core * half_o, 16), half_o), pl.ds(lo, count)
        ]

    gather_o = Gather(
        wo_mine.at[pl.ds(pl.multiple_of(c * half_o, 16), half_o)],
        wo_part(c, 0, width), wo_part(c, 0, width // 2), wo_part(c, width // 2, width // 2), o_send, o_recv,
    )

    def partner_copy(sl, core):
        region = wo_part(core, 0, width)(sl)
        return remote(region, region, p_send.at[sl], p_recv.at[sl], s, head_of(0, 1 - c))

    got_wq.wait()
    for gather_q in gathers_q:
        gather_q.start_a()
        gather_q.start_b()
    got_hidden.wait()

    def row_block(dy, core, offset=0, count=own):
        return rows.at[lax.rem(y + dy + 4, 4), pl.ds(pl.multiple_of(core * own + offset, 16), count)]

    def norm_rows(i, carry):
        values = hidden[pl.ds(pl.multiple_of(i * 32, 32), 32), :].astype(F32)
        meansq = jnp.mean(values * values, axis=-1, keepdims=True)
        normed = (values * lax.rsqrt(meansq + 1e-05) * gain[...].reshape(1, width)).astype(BF16)
        rows[y, pl.ds(pl.multiple_of(c * own + i * 32, 32), 32), :] = normed
        return carry


    def y_copy(m, region, dy, core):
        return remote(region, region, y_send.at[m], y_recv.at[m], s, head_of(dy, core))

    half = own // 2
    lax.fori_loop(0, half // 32, norm_rows, 0)
    y_copy(1, row_block(0, c, 0, half), 1, c).start()
    lax.fori_loop(half // 32, own // 32, norm_rows, 0)
    y_copy(3, row_block(0, c, half, half), -1, c).start()
    y_copy(2, row_block(0, c, half, half), 1, c).start()
    y_copy(4, row_block(0, c, 0, half), -1, c).start()
    y_copy(0, row_block(0, c), 0, 1 - c).start()

    for gather_q in gathers_q:
        gather_q.second_step()
    got_keys.wait()

    def prepare_cache(i, carry):
        at = pl.ds(pl.multiple_of(i * 256, 256), 256)
        token = i * 256 + lax.broadcasted_iota(jnp.int32, (48, 256), 1)
        first = lax.broadcasted_iota(jnp.int32, (48, 256), 0) == 0
        bias = jnp.where(first & (token < WINDOW - prefix), HIDE, 0.0)
        block = jnp.transpose(jnp.concatenate([cached_keys[:, at].astype(F32), bias], axis=0))
        lane = lax.broadcasted_iota(jnp.int32, (256, 128), 1)
        keys[at, :128] = block.astype(BF16)
        keys[at, 128:] = jnp.where(lane < HEAD_DIM, block, 0.0).astype(BF16)
        return carry

    lax.fori_loop(0, WINDOW // 256, prepare_cache, 0)
    for gather_q in gathers_q:
        gather_q.third_step()
    got_wo.wait()
    got_vals.wait()
    got_cos.wait()
    got_sin.wait()
    total = vals.shape[1]
    one_row = (lax.broadcasted_iota(jnp.int32, (16, 512), 0) == 0).astype(F32).astype(BF16)
    for i in range(total // 512):
        vals[HEAD_DIM:, i * 512 : (i + 1) * 512] = one_row
    for k in range(4):
        for i in range(3):
            cols = slice(i * 512, (i + 1) * 512)
            queries[k, 80:96, cols] = one_row
            queries[k, 96:128, cols] = jnp.zeros((32, 512), BF16)
            queries[k, 208:256, cols] = jnp.zeros((48, 512), BF16)
    turn_pre = frequency[...] * prefix.astype(F32)
    cp, sp = jnp.cos(turn_pre)[:, 0:1], jnp.sin(turn_pre)[:, 0:1]

    for gather_q in gathers_q:
        gather_q.fourth_step(range(4))
    gather_o.start_a()
    y_copy(0, row_block(0, 1 - c), 0, c).wait_recv()
    y_copy(1, row_block(-1, c, 0, half), 0, c).wait_recv()
    y_copy(5, row_block(-1, c, 0, half), 1, c).start()
    y_copy(3, row_block(1, c, half, half), 0, c).wait_recv()
    y_copy(6, row_block(1, c, half, half), -1, c).start()
    y_copy(7, row_block(-1, c, 0, half), 0, 1 - c).start()
    y_copy(9, row_block(1, c, half, half), 0, 1 - c).start()
    for gather_q in gathers_q:
        gather_q.last_step()
    gather_o.start_b()

    scale = math.log2(math.e) / math.sqrt(HEAD_DIM)

    def project(yk):
        projected = jnp.transpose(matmul(rows[yk], wq[...]))
        tokens = pl.ds(pl.multiple_of(yk * chip, 128), chip)
        cn, sn = cos_slot[:, tokens], sin_slot[:, tokens]
        cosine, sine = cn * cp - sn * sp, sn * cp + cn * sp

        def rotate(at):
            lead, trail = projected[at : at + HALF], projected[at + HALF : at + HEAD_DIM]
            turned = jnp.concatenate([lead * cosine - trail * sine, trail * cosine + lead * sine], axis=0)
            return turned.astype(BF16).astype(F32)

        for g in range(GROUP):
            scaled = rotate(g * HEAD_DIM) * scale
            high = scaled.astype(BF16)
            low = (scaled - high.astype(F32)).astype(BF16)
            for j in range(3):
                cols = slice(j * 512 + g * 128, j * 512 + g * 128 + 128)
                toks = slice(j * 128, j * 128 + 128)
                queries[yk, 0:80, cols] = high[:, toks]
                queries[yk, 128:208, cols] = low[:, toks]
        key = rotate(GROUP * HEAD_DIM)
        value = projected[(GROUP + 1) * HEAD_DIM : (GROUP + 2) * HEAD_DIM].astype(BF16)
        slots = pl.ds(pl.multiple_of(WINDOW + yk * chip, 128), chip)
        vals[:HEAD_DIM, slots] = value
        pair = jnp.concatenate([key, value.astype(F32)], axis=0)
        index = yk * chip + lax.broadcasted_iota(jnp.int32, pair.shape, 1)
        written[:, tokens] = jnp.where(index < length, pair, 0.0).astype(BF16)
        clean = jnp.transpose(jnp.concatenate([key, jnp.zeros((48, chip), F32)], axis=0)).astype(BF16)
        keys[slots, :128] = clean
        keys[slots, 128:] = clean

    def scores(start, count, block_queries):
        return matmul(keys[pl.ds(pl.multiple_of(start, 128), count), :], block_queries)

    def absorb(carry, sc, parts):
        peak, total_ = carry
        top = jnp.max(sc, axis=0, keepdims=True)
        if peak is not None:
            top = jnp.maximum(peak, top)
        weights = jnp.exp2(sc - top).astype(BF16)
        if peak is not None:
            total_ = total_ * jnp.exp2(peak - top)
        at = 0
        for start, count in parts:
            add = matmul(vals[:88, pl.ds(pl.multiple_of(start, 128), count)], weights[at : at + count])
            total_ = add if total_ is None else total_ + add
            at += count
        return top, total_

    common = 4 * chip

    def first_phase(yk):
        keys_at = range(common, WINDOW, KEYS1)
        todo = [(at, start) for at in range(0, 4 * chip, COLS1) for start in keys_at]

        def make(t):
            at, start = todo[t]
            return scores(start, KEYS1, queries[yk, :, at : at + COLS1])

        sc = make(0)
        carry = (None, None)
        for t, (at, start) in enumerate(todo):
            later = make(t + 1) if t + 1 < len(todo) else None
            carry = absorb(carry, sc, [(start, KEYS1)])
            if start + KEYS1 == WINDOW:
                maxes[yk, :, at : at + COLS1] = carry[0]
                state[yk, :, at : at + COLS1] = carry[1]
                carry = (None, None)
            sc = later

    def second_phase(yk):
        base = yk * chip
        full = [
            jnp.where(yk + i < 3, base + (i + 1) * chip, WINDOW + (i - (3 - yk)) * chip) for i in range(3)
        ]

        def make(j, u):
            block_queries = queries[yk, :, j * 512 : (j + 1) * 512]
            if u < 3:
                return scores(full[u], chip, block_queries)
            lowest, upto = chip - j * 128, (j + 1) * 128
            row = lax.broadcasted_iota(jnp.int32, (128, 512), 0)
            col = lax.broadcasted_iota(jnp.int32, (128, 512), 1) & (QBLOCK - 1)
            low = scores(base + j * 128, lowest, block_queries)
            high = scores(WINDOW + base, upto, block_queries)
            parts = [jnp.where(row > col, low[:128], HIDE), low[128:], high[:-128], jnp.where(row <= col, high[-128:], HIDE)]
            return jnp.concatenate([p for p in parts if p.shape[0]], axis=0)

        units = [(j, u) for j in range(3) for u in range(4)]
        sc = make(*units[0])
        for t, (j, u) in enumerate(units):
            later = make(*units[t + 1]) if t + 1 < len(units) else None
            cols = slice(j * 512, (j + 1) * 512)
            if u == 0:
                carry = (maxes[yk, :, cols], state[yk, :, cols])
            if u < 3:
                parts = [(full[u], chip)]
            else:
                parts = [(base + j * 128, chip - j * 128), (WINDOW + base, (j + 1) * 128)]
            carry = absorb(carry, sc, parts)
            if u == 3:
                sums = carry[1]
                attended = sums[:HEAD_DIM] * (1.0 / sums[HEAD_DIM : HEAD_DIM + 1])
                token = base + j * 128 + (lax.broadcasted_iota(jnp.int32, (HEAD_DIM, 512), 1) & (QBLOCK - 1))
                attended = jnp.where(token < length, attended, 0.0)
                heads = [attended[:, g * 128 : (g + 1) * 128] for g in range(GROUP)]
                if j == 1:
                    left = lax.broadcasted_iota(jnp.int32, (HEAD_DIM, 128), 1) < 64
                    for p in range(2):
                        one, two = heads[p], heads[p + 2]
                        at = slice(320 + p * HEAD_DIM, 320 + (p + 1) * HEAD_DIM)
                        ready[yk, 0, at, :] = jnp.where(left, one, pltpu.roll(two, 64, 1)).astype(BF16)
                        ready[yk, 1, at, :] = jnp.where(left, pltpu.roll(one, 64, 1), two).astype(BF16)
                else:
                    for g in range(GROUP):
                        ready[yk, j // 2, g * HEAD_DIM : (g + 1) * HEAD_DIM, :] = heads[g].astype(BF16)
            sc = later

    def arrive(k):
        @pl.when(k == 1)
        def _():
            y_copy(2, row_block(-1, c, half, half), 0, c).wait_recv()
            y_copy(8, row_block(-1, c, half, half), 0, 1 - c).start()
            y_copy(4, row_block(1, c, 0, half), 0, c).wait_recv()
            y_copy(10, row_block(1, c, 0, half), 0, 1 - c).start()
            gather_o.second_step()
            y_copy(7, row_block(-1, 1 - c, 0, half), 0, c).wait_recv()
            y_copy(8, row_block(-1, 1 - c, half, half), 0, c).wait_recv()

        @pl.when(k == 2)
        def _():
            gather_o.third_step()
            y_copy(9, row_block(1, 1 - c, half, half), 0, c).wait_recv()
            y_copy(10, row_block(1, 1 - c, 0, half), 0, c).wait_recv()

        @pl.when(k == 3)
        def _():
            y_copy(5, row_block(2, c, 0, half), 0, c).wait_recv()
            y_copy(6, row_block(2, c, half, half), 0, c).wait_recv()
            y_copy(11, row_block(2, c), 0, 1 - c).start()
            gather_o.fourth_step((0,))
            for q in range(1, 4):
                partner_copy(slot(turns[q], 0), c).start()
            y_copy(11, row_block(2, 1 - c), 0, c).wait_recv()

    def first_loop(k, carry):
        arrive(k)
        turn = jnp.where(k == 0, 0, jnp.where(k == 1, 3, k - 1))
        yk = lax.rem(y + turn, 4)
        project(yk)
        first_phase(yk)
        return carry

    lax.fori_loop(0, 4, first_loop, 0)

    def attended_copy(yk, core):
        return remote(
            ready.at[yk, core], received.at[h], a_send.at[2 * yk + core], a_recv.at[h], s, 2 * yk + core
        )

    def second_loop(k, carry):
        turn = jnp.where(k == 0, 2, jnp.where(k == 1, 1, jnp.where(k == 2, 3, 0)))
        yk = lax.rem(y + turn, 4)

        @pl.when(k == 0)
        def _():
            gather_o.fourth_step((1, 2))

        @pl.when(k == 1)
        def _():
            gather_o.fourth_step((3,))
            for q in range(4):
                partner_copy(slot(turns[q], -1), c).start()
                partner_copy(slot(turns[q], 1), c).start()

        @pl.when(k == 3)
        def _():
            gather_o.last_step()
            for q in range(4):
                partner_copy(slot(turns[q], 2), c).start()

        second_phase(yk)

        @pl.when(k < 3)
        def _():
            attended_copy(yk, 0).start()
            attended_copy(yk, 1).start()

        @pl.when(k == 3)
        def _():
            attended_copy(yk, 1 - c).start()

        return carry

    lax.fori_loop(0, 4, second_loop, 0)

    def unpack(src_head, block):
        top = src_head * GROUP * HEAD_DIM
        landed[pl.ds(pl.multiple_of(top, 16), GROUP * HEAD_DIM), :128] = block[: GROUP * HEAD_DIM]
        packed = block[GROUP * HEAD_DIM :]
        landed[pl.ds(pl.multiple_of(top, 16), 2 * HEAD_DIM), 128:] = packed
        turned_back = pltpu.roll(packed.astype(F32), 64, 1).astype(BF16)
        landed[pl.ds(pl.multiple_of(top + 2 * HEAD_DIM, 16), 2 * HEAD_DIM), 128:] = turned_back

    unpack(h, ready[y, c])

    for dy, core in ((0, 1 - c), (2, 0), (2, 1), (1, 0), (1, 1), (-1, 0), (-1, 1)):
        src = head_of(dy, core)
        remote(received.at[src], received.at[src], a_send.at[0], a_recv.at[src], s, h).wait_recv()
        unpack(src, received[src])
    for d in range(1, 16):
        sl = lax.rem(s + d, 16)
        partner_copy(sl, 1 - c).wait_recv()
    for i in range(width // 512):
        turned[:, i * 512 : (i + 1) * 512] = jnp.transpose(matmul(wo[i * 512 : (i + 1) * 512, :], landed[...]))
    rest = own - 128
    out[pl.ds(pl.multiple_of(c * rest, 64), 128), :] = turned[:128, :].astype(BF16)
    out[pl.ds(pl.multiple_of((1 - c) * 128, 64), rest), :] = turned[128:own, :].astype(BF16)

    for gather_q in gathers_q:
        gather_q.drain()
    gather_o.drain()
    for d in range(1, 16):
        partner_copy(lax.rem(s + d, 16), c).wait_send()
    for m in (0, 11):
        y_copy(m, row_block(0, c), 0, 1 - c).wait_send()
    for m in range(1, 11):
        y_copy(m, row_block(0, c, 0, half), 0, 1 - c).wait_send()
    for d in range(1, 8):
        dst = lax.rem(h + d, 8)
        remote(received.at[0], received.at[0], a_send.at[dst], a_recv.at[0], s, dst).wait_send()


def solution(mesh):
    def step(hidden, norm_gain, w_qkv, w_out, kv_cache, new_len, prefix_len):
        s, h = lax.axis_index("seq"), lax.axis_index("head")
        own, width = hidden.shape[1], hidden.shape[2]
        new_total = 8 * own
        wide = (GROUP + 2) * HEAD_DIM
        piece = w_qkv.shape[0]
        w_mine = lax.dynamic_slice(w_qkv, (0, h * wide), (piece, wide))
        wo_mine = w_out.T
        cached = jnp.swapaxes(kv_cache.reshape(WINDOW, 2 * HEAD_DIM), 0, 1)
        frequency = np.exp(np.arange(HALF, dtype=np.float64) * (-2.0 * math.log(10000.0) / HEAD_DIM))
        angles = frequency[:, None] * np.arange(new_total, dtype=np.float64)[None, :]
        cos_slot = jnp.asarray(np.cos(angles).astype(np.float32))
        sin_slot = jnp.asarray(np.sin(angles).astype(np.float32))
        lanes = jnp.asarray(np.broadcast_to(frequency[:, None], (HALF, 128)).astype(np.float32))
        chip = 2 * own
        dma = pltpu.SemaphoreType.DMA
        vmem = pl.BlockSpec(memory_space=pltpu.VMEM)
        smem = pl.BlockSpec(memory_space=pltpu.SMEM)
        any_ = pl.BlockSpec(memory_space=pl.ANY)
        attn_out, kv_written = pl.pallas_call(
            kernel,
            out_shape=(
                pltpu.VMEM((own, width), BF16),
                pltpu.VMEM((2 * HEAD_DIM, new_total), BF16),
            ),
            in_specs=[any_, vmem, any_, any_, any_, any_, any_, vmem, smem, smem],
            out_specs=(vmem, vmem),
            scratch_shapes=[
                pltpu.VMEM((own, width), BF16),
                pltpu.VMEM((HALF, new_total), F32),
                pltpu.VMEM((HALF, new_total), F32),
                pltpu.VMEM((HEAD_DIM, WINDOW), BF16),
                pltpu.VMEM((4, chip, width), BF16),
                pltpu.VMEM((16 * piece, wide), BF16),
                pltpu.VMEM((16 * piece, width), BF16),
                pltpu.VMEM((WINDOW + new_total, 256), BF16),
                pltpu.VMEM((96, WINDOW + new_total), BF16),
                pltpu.VMEM((4, 256, 4 * chip), BF16),
                pltpu.VMEM((4, 88, 4 * chip), F32),
                pltpu.VMEM((4, 1, 4 * chip), F32),
                pltpu.VMEM((4, 2, 6 * HEAD_DIM, 128), BF16),
                pltpu.VMEM((8, 6 * HEAD_DIM, 128), BF16),
                pltpu.VMEM((8 * GROUP * HEAD_DIM, 256), BF16),
                pltpu.VMEM((256, width), F32),
                dma((7,)), dma((20 * len(SPLITS),)), dma((20 * len(SPLITS),)), dma((20,)), dma((20,)), dma((16,)), dma((16,)),
                dma((12,)), dma((12,)), dma((8,)), dma((8,)),
            ],
            compiler_params=pltpu.CompilerParams(
                collective_id=0, has_side_effects=True, vmem_limit_bytes=56 * 1024 * 1024
            ),
        )(
            hidden.reshape(own, width), norm_gain, w_mine, wo_mine,
            cached, cos_slot, sin_slot, lanes, new_len, prefix_len,
        )
        return attn_out.reshape(1, own, width), jnp.swapaxes(kv_written, 0, 1).reshape(1, new_total, 2 * HEAD_DIM)

    return jax.shard_map(
        step,
        mesh=mesh,
        in_specs=(
            P("seq", "head", None), P(), P("seq", None), P(None, "seq"), P("seq", None, "head"), P(), P(),
        ),
        out_specs=(P("seq", "head", None), P("seq", None, "head")),
        check_vma=False,
    )
```
